32 devices in a mesh: dom: 16 (over z, x, core), col: 2 (over y).
Axes of the slice: x: 2, y: 2, z: 4, core: 2. Of those that a mesh axis runs over, the one named last changes fastest.
Arguments:
- snapshots: bfloat16 [128, 3, 32768], P('col', None, 'dom'), may hold values from -30 to 30
- mass_tiles: bfloat16 [16, 3, 3, 32768], P(None, None, None, 'dom'), may hold values from -2 to 2
- tile_slot: int32 [15, 32768], P(None, 'dom'), may hold values from 0 to 3071
- send_up: int32 [8192], P('dom'), may hold values from 0 to 2047
- send_down: int32 [8192], P('dom'), may hold values from 0 to 2047
Outputs:
- mass_snap: bfloat16 [128, 3, 32768], P('col', None, 'dom')
- gram: float32 [128, 128], P(None, 'col')
The draws below stay inside these ranges and needn't reach their ends.
Inputs may be any that keep to these rules, and one draw needn't show every extreme that they name: `tile_slot`: slots below 2048 are the partition's own nodes, the next 512 those received from the previous partition, the last 512 those from the next partition.
All inputs are finite; a program needn't handle non-finite values.
Results may differ from the reference program's by a relative error of at most 0.001.
Values may be sent and summed in bfloat16 or wider, within the bound.
No kernel may reach another device: no remote copies, remote signals or barrier semaphores. Data moves between devices by JAX's collectives and lax.ppermute only.
A program may use at most 64 MiB of HBM per device.

```python
import jax
import jax.numpy as jnp
from jax import lax

NSNAP = 128
TILES = 16
NODES_DEV = 2048
HALO = 512
NODES = 32768
HALO_ALL = 8192
N_DOM = 16


def draw_snapshots(key, part):
    key_common = jax.random.fold_in(key, 11)
    key_fluct = jax.random.fold_in(key, 12)
    key_scale = jax.random.fold_in(key, 13)
    position = jnp.arange(NODES, dtype=jnp.float32) / max(NODES - 1, 1)
    node_weight = 0.6 * jnp.exp(position * jnp.log(3.0))
    common = jnp.clip(jax.random.normal(key_common, (3, NODES), jnp.float32), -4.0, 4.0)
    fluct = jnp.clip(jax.random.normal(key_fluct, (NSNAP, 3, NODES), jnp.float32), -4.0, 4.0)
    snap_scale = jnp.exp(jax.random.uniform(key_scale, (NSNAP, 1, 1), jnp.float32, jnp.log(0.3), jnp.log(3.0)))
    values = node_weight[None, None, :] * (common[None] + snap_scale * fluct)
    return values.astype(jnp.bfloat16)


def draw_mass_tiles(key, part):
    key_off = jax.random.fold_in(key, 21)
    key_diag = jax.random.fold_in(key, 22)
    off_diag = 0.07 * jnp.clip(jax.random.normal(key_off, (TILES, 3, 3, NODES), jnp.float32), -4.0, 4.0)
    diag_vals = jax.random.uniform(key_diag, (3, NODES), jnp.float32, 0.5, 1.5)
    comp_ids = jnp.arange(3)
    identity = (comp_ids[:, None] == comp_ids[None, :]).astype(jnp.float32)
    tile_ids = jnp.arange(TILES)
    first_tile = (tile_ids == 0).astype(jnp.float32)
    values = off_diag + first_tile[:, None, None, None] * identity[None, :, :, None] * diag_vals[None, :, None, :]
    return values.astype(jnp.bfloat16)


def touch_ends(drawn, rng, smallest, largest):
    extent = drawn.shape
    spot = [jax.random.randint(jax.random.fold_in(rng, axis), (), 0, extent[axis]) for axis in range(len(extent))]
    drawn = drawn.at[tuple(spot)].set(smallest)
    longest = extent.index(max(extent))
    spot[longest] = (spot[longest] + 1) % extent[longest]
    return drawn.at[tuple(spot)].set(largest)


def setup_inputs(seed: int = 0) -> dict:
    streams_of = jax.random.split(jax.random.key(seed), 6)
    return {
        "snapshots": draw_snapshots(jax.random.fold_in(streams_of[5], 71), 0),
        "mass_tiles": draw_mass_tiles(jax.random.fold_in(streams_of[5], 71), 0),
        "tile_slot": touch_ends(jax.random.randint(streams_of[2], (TILES - 1, NODES), 0, NODES_DEV + 2 * HALO), jax.random.fold_in(streams_of[2], 1), 0, (NODES_DEV + 2 * HALO) - 1).astype(jnp.int32),
        "send_up": touch_ends(jax.random.randint(streams_of[3], (HALO_ALL,), 0, NODES_DEV), jax.random.fold_in(streams_of[3], 1), 0, NODES_DEV - 1).astype(jnp.int32),
        "send_down": touch_ends(jax.random.randint(streams_of[4], (HALO_ALL,), 0, NODES_DEV), jax.random.fold_in(streams_of[4], 1), 0, NODES_DEV - 1).astype(jnp.int32),
    }


def couple(tiles, values):
    total_sum = tiles[None, :, 0, :].astype(jnp.float32) * values[:, None, 0, :].astype(jnp.float32)
    for in_comp in (1, 2):
        total_sum = total_sum + tiles[None, :, in_comp, :].astype(jnp.float32) * values[:, None, in_comp, :].astype(jnp.float32)
    return total_sum


def reference(snapshots, mass_tiles, tile_slot, send_up, send_down):
    parts = snapshots.reshape(NSNAP, 3, N_DOM, NODES_DEV)
    up_lists = send_up.reshape(N_DOM, HALO)[None, None]
    down_lists = send_down.reshape(N_DOM, HALO)[None, None]
    up_sent = jnp.take_along_axis(parts, up_lists, axis=3)
    down_sent = jnp.take_along_axis(parts, down_lists, axis=3)
    zero_rim = jnp.zeros((NSNAP, 3, 1, HALO), jnp.bfloat16)
    from_lower = jnp.concatenate([zero_rim, up_sent[:, :, :-1]], axis=2)
    from_upper = jnp.concatenate([down_sent[:, :, 1:], zero_rim], axis=2)
    extended = jnp.concatenate([parts, from_lower, from_upper], axis=3)
    slot_parts = tile_slot.reshape(TILES - 1, N_DOM, NODES_DEV)
    first_term = couple(mass_tiles[0], snapshots)

    def add_tile(tile_index, total_sum):
        tiles = lax.dynamic_index_in_dim(mass_tiles, tile_index, 0, keepdims=False)
        slots = lax.dynamic_index_in_dim(slot_parts, tile_index - 1, 0, keepdims=False)
        neighbour_vals = jnp.take_along_axis(extended, slots[None, None], axis=3)
        return total_sum + couple(tiles, neighbour_vals.reshape(NSNAP, 3, NODES))

    mass_snap = lax.fori_loop(1, TILES, add_tile, first_term).astype(jnp.bfloat16)
    flat_snap = snapshots.reshape(NSNAP, 3 * NODES)
    flat_mass = mass_snap.reshape(NSNAP, 3 * NODES)
    gram = lax.dot_general(flat_snap, flat_mass, (((1,), (1,)), ((), ())), preferred_element_type=jnp.float32)
    gram = gram / (3.0 * NODES)
    return mass_snap, gram
```

```python
import functools

import jax
import jax.numpy as jnp
import numpy as np
from jax import lax
from jax.experimental import pallas as pl
from jax.experimental.pallas import tpu as pltpu
from jax.sharding import PartitionSpec as P

LANES = 128
HALF = LANES // 2
GROUP = 8
BF16 = jnp.bfloat16
F32 = jnp.float32


def shifted(value, axis, steps):
    count = lax.axis_size(axis)
    leading, last = (max(0, -steps), min(count, count - steps))
    return lax.ppermute(value, axis, [(source, source + steps) for source in range(leading, last)])


def nt_dot(left, right):
    return lax.dot_general(left, right, (((1,), (1,)), ((), ())), preferred_element_type=F32)


def table_kernel(snap_ref, up_ref, down_ref, table_ref, to_upper_ref, to_lower_ref):
    node_count = snap_ref.shape[2]
    row = lax.broadcasted_iota(jnp.int32, (2 * LANES, 2 * LANES), 0)
    col = lax.broadcasted_iota(jnp.int32, (2 * LANES, 2 * LANES), 1)
    pick = jnp.where(col == (row // 2) + LANES * (row % 2), 1.0, 0.0).astype(BF16)
    empty = jnp.zeros((HALF, LANES), BF16)
    for start in range(0, node_count, LANES):
        comps = [snap_ref[:, comp, start : start + LANES] for comp in range(3)]
        first = jnp.concatenate([comps[0], comps[2]], axis=0)
        second = jnp.concatenate([comps[1], empty], axis=0)
        rows = nt_dot(pick, jnp.concatenate([first, second], axis=1)).astype(BF16)
        table_ref[start : start + LANES] = rows.reshape(LANES, 2, LANES)
    for out_ref, list_ref in ((to_upper_ref, up_ref), (to_lower_ref, down_ref)):
        for entry in range(out_ref.shape[0]):
            out_ref[entry] = table_ref[list_ref[entry]]


def node_table(snap, send_up, send_down):
    node_count = snap.shape[2]
    halo = send_up.shape[0]
    smem = pl.BlockSpec(memory_space=pltpu.SMEM)
    vmem = pl.BlockSpec(memory_space=pltpu.VMEM)
    return pl.pallas_call(
        table_kernel,
        in_specs=[vmem, smem, smem],
        out_specs=[vmem] * 3,
        out_shape=[
            jax.ShapeDtypeStruct((node_count, 2, LANES), BF16),
            jax.ShapeDtypeStruct((halo, 2, LANES), BF16),
            jax.ShapeDtypeStruct((halo, 2, LANES), BF16),
        ],
        name="node_table",
    )(snap, send_up, send_down)


def spread_matrix(tiles):
    spread = np.zeros((tiles, 3, 3, 2, 3, tiles, GROUP, 2), np.float32)
    for tile in range(tiles):
        for comp in range(3):
            for half, pair, in_comp in ((0, 0, 0), (0, 1, 1), (1, 0, 2)):
                spread[tile, comp, in_comp, half, comp, tile, :, pair] = 1.0
    return jnp.asarray(spread.reshape(tiles * 9, 6 * tiles * GROUP * 2), BF16)


def spread_kernel(tile_ref, spread_ref, out_ref):
    depth = out_ref.shape[2]
    turned = tile_ref[...].astype(F32).T.astype(BF16)
    node = lax.broadcasted_iota(jnp.int32, (GROUP, depth), 0)
    slot = (lax.broadcasted_iota(jnp.int32, (GROUP, depth), 1) // 2) % GROUP
    own = node == slot
    for pair in range(3):
        both = [
            jnp.dot(turned, spread_ref[:, (2 * pair + one) * depth : (2 * pair + one + 1) * depth], preferred_element_type=F32)
            for one in range(2)
        ]
        for group in range(out_ref.shape[0]):
            kept = [jnp.where(own, part[group * GROUP : (group + 1) * GROUP], 0.0) for part in both]
            out_ref[group, 16 * pair : 16 * (pair + 1), :] = jnp.concatenate(kept, axis=0).astype(BF16)


def spread_tiles(mass_tiles):
    tiles, _, _, node_count = mass_tiles.shape
    depth = tiles * GROUP * 2
    step = LANES
    spread = spread_matrix(tiles)
    return pl.pallas_call(
        spread_kernel,
        grid=(node_count // step,),
        in_specs=[
            pl.BlockSpec((tiles * 9, step), lambda i: (0, i)),
            pl.BlockSpec(spread.shape, lambda i: (0, 0)),
        ],
        out_specs=pl.BlockSpec((step // GROUP, 48, depth), lambda i: (i, 0, 0)),
        out_shape=jax.ShapeDtypeStruct((node_count // GROUP, 48, depth), BF16),
        cost_estimate=pl.CostEstimate(flops=2 * node_count * tiles * 9 * 6 * depth, bytes_accessed=node_count * 6 * depth * 2, transcendentals=0),
        name="spread_tiles",
    )(mass_tiles.reshape(tiles * 9, node_count), spread)


def mass_kernel(slot_hbm, table_hbm, lower_hbm, upper_hbm, left_ref, out_ref, slots0, slots1, table_ref, turn_ref, sem, fill_sem):
    step, steps = pl.program_id(0), pl.num_programs(0)
    others = slot_hbm.shape[0]
    nodes, halo = table_hbm.shape[0], lower_hbm.shape[0]
    low_half = lax.broadcasted_iota(jnp.int32, (GROUP, LANES), 1) < HALF
    slot_refs = (slots0, slots1)

    def fetch(block, part):
        source = slot_hbm.at[:, pl.ds(pl.multiple_of(block * LANES, LANES), LANES)]
        return pltpu.make_async_copy(source, slot_refs[part], sem.at[part])

    @pl.when(step == 0)
    def _():
        fetch(0, 0).start()
        fetch(1, 1).start()
        fills = [
            pltpu.make_async_copy(table_hbm, table_ref.at[pl.ds(0, nodes)], fill_sem.at[0]),
            pltpu.make_async_copy(lower_hbm, table_ref.at[pl.ds(nodes, halo)], fill_sem.at[1]),
            pltpu.make_async_copy(upper_hbm, table_ref.at[pl.ds(nodes + halo, halo)], fill_sem.at[2]),
        ]
        for fill in fills:
            fill.start()
        for fill in fills:
            fill.wait()

    for part in range(2):
        block = 2 * step + part
        fetch(block, part).wait()
        for group in range(LANES // GROUP):
            first = block * LANES + group * GROUP
            rows = [table_ref[pl.ds(first, GROUP)].reshape(2 * GROUP, LANES)]
            for tile in range(others):
                found = [table_ref[slot_refs[part][tile, group * GROUP + node]] for node in range(GROUP)]
                rows.append(jnp.stack(found).reshape(2 * GROUP, LANES))
            sums = jnp.dot(left_ref[part * (LANES // GROUP) + group], jnp.concatenate(rows, axis=0), preferred_element_type=F32)
            for comp in range(3):
                low = sums[comp * GROUP : (comp + 1) * GROUP]
                high = sums[(3 + comp) * GROUP : (4 + comp) * GROUP]
                turn_ref[comp, group * GROUP : (group + 1) * GROUP, :] = jnp.where(low_half, low, high)

        @pl.when(step < steps - 1)
        def _():
            fetch(block + 2, part).start()

        for comp in range(3):
            turned = turn_ref[comp].T
            out_ref[:, comp, part * LANES : (part + 1) * LANES] = (turned[:HALF] + turned[HALF:]).astype(BF16)


def apply_mass(table, from_lower, from_upper, left, tile_slot):
    nodes, halo = table.shape[0], from_lower.shape[0]
    others = tile_slot.shape[0]
    any_space = pl.BlockSpec(memory_space=pl.ANY)
    groups = 2 * LANES // GROUP
    return pl.pallas_call(
        mass_kernel,
        grid=(nodes // (2 * LANES),),
        in_specs=[any_space] * 4 + [pl.BlockSpec((groups, 48, left.shape[2]), lambda i: (i, 0, 0))],
        out_specs=pl.BlockSpec((HALF, 3, 2 * LANES), lambda i: (0, 0, i)),
        out_shape=jax.ShapeDtypeStruct((HALF, 3, nodes), BF16),
        scratch_shapes=[
            pltpu.SMEM((others, LANES), jnp.int32),
            pltpu.SMEM((others, LANES), jnp.int32),
            pltpu.VMEM((nodes + 2 * halo, 2, LANES), BF16),
            pltpu.VMEM((3, LANES, LANES), F32),
            pltpu.SemaphoreType.DMA((2,)),
            pltpu.SemaphoreType.DMA((3,)),
        ],
        cost_estimate=pl.CostEstimate(flops=2 * nodes * 6 * left.shape[2] * LANES, bytes_accessed=left.size * 2, transcendentals=0),
        name="mass_rows",
    )(tile_slot, table, from_lower, from_upper, left)


def summed(value, axis):
    count = lax.axis_size(axis)
    if count & (count - 1):
        return lax.psum(value, axis)
    step = 1
    while step < count:
        value = value + lax.ppermute(value, axis, [(source, source ^ step) for source in range(count)])
        step *= 2
    return value


def body(snapshots, mass_tiles, tile_slot, send_up, send_down):
    snap_count, _, node_count = snapshots.shape
    cols = lax.axis_size("col")
    others = [
        lax.ppermute(snapshots, "col", [(source, (source + shift) % cols) for source in range(cols)])
        for shift in range(1, cols)
    ]
    left = spread_tiles(mass_tiles)
    pieces = []
    for start in range(0, snap_count, HALF):
        piece = snapshots[start : start + HALF]
        size = piece.shape[0]
        if size < HALF:
            piece = jnp.pad(piece, ((0, HALF - size), (0, 0), (0, 0)))
        table, to_upper, to_lower = node_table(piece, send_up, send_down)
        from_lower = shifted(to_upper, "dom", 1)
        from_upper = shifted(to_lower, "dom", -1)
        pieces.append(apply_mass(table, from_lower, from_upper, left, tile_slot)[:size])
    mass_snap = pieces[0] if len(pieces) == 1 else jnp.concatenate(pieces, axis=0)
    flat_mass = mass_snap.reshape(snap_count, -1)
    terms = jnp.concatenate([nt_dot(part.reshape(snap_count, -1), flat_mass) for part in [snapshots] + others], axis=0)
    total = summed(terms, "dom") / (3.0 * node_count * lax.axis_size("dom"))
    gram = jnp.roll(total.reshape(cols, snap_count, snap_count)[::-1], lax.axis_index("col") + 1, axis=0)
    return mass_snap, gram.reshape(cols * snap_count, snap_count)


def solution(mesh):
    placed = (P("col", None, "dom"), P(None, None, None, "dom"), P(None, "dom"), P("dom"), P("dom"))
    return jax.shard_map(
        body,
        mesh=mesh,
        in_specs=placed,
        out_specs=(P("col", None, "dom"), P(None, "col")),
        check_vma=False,
    )
```

```python
import functools

import jax
import jax.numpy as jnp
import numpy as np
from jax import lax
from jax.experimental import pallas as pl
from jax.experimental.pallas import tpu as pltpu
from jax.sharding import PartitionSpec as P

LANES = 128
HALF = LANES // 2
GROUP = 8
BF16 = jnp.bfloat16
F32 = jnp.float32


def shifted(value, axis, steps):
    count = lax.axis_size(axis)
    leading, last = (max(0, -steps), min(count, count - steps))
    return lax.ppermute(value, axis, [(source, source + steps) for source in range(leading, last)])


def nt_dot(left, right):
    return lax.dot_general(left, right, (((1,), (1,)), ((), ())), preferred_element_type=F32)


def table_kernel(snap_ref, up_ref, down_ref, table_ref, to_upper_ref, to_lower_ref):
    node_count = snap_ref.shape[2]
    row = lax.broadcasted_iota(jnp.int32, (2 * LANES, 2 * LANES), 0)
    col = lax.broadcasted_iota(jnp.int32, (2 * LANES, 2 * LANES), 1)
    pick = jnp.where(col == (row // 2) + LANES * (row % 2), 1.0, 0.0).astype(BF16)
    empty = jnp.zeros((HALF, LANES), BF16)
    for start in range(0, node_count, LANES):
        comps = [snap_ref[comp, :, start : start + LANES] for comp in range(3)]
        first = jnp.concatenate([comps[0], comps[2]], axis=0)
        second = jnp.concatenate([comps[1], empty], axis=0)
        rows = nt_dot(pick, jnp.concatenate([first, second], axis=1)).astype(BF16)
        table_ref[start : start + LANES] = rows.reshape(LANES, 2, LANES)
    for out_ref, list_ref in ((to_upper_ref, up_ref), (to_lower_ref, down_ref)):
        for entry in range(out_ref.shape[0]):
            out_ref[entry] = table_ref[list_ref[entry]]


def node_table(snap, send_up, send_down):
    node_count = snap.shape[2]
    halo = send_up.shape[0]
    smem = pl.BlockSpec(memory_space=pltpu.SMEM)
    vmem = pl.BlockSpec(memory_space=pltpu.VMEM)
    return pl.pallas_call(
        table_kernel,
        in_specs=[vmem, smem, smem],
        out_specs=[vmem] * 3,
        out_shape=[
            jax.ShapeDtypeStruct((node_count, 2, LANES), BF16),
            jax.ShapeDtypeStruct((halo, 2, LANES), BF16),
            jax.ShapeDtypeStruct((halo, 2, LANES), BF16),
        ],
        name="node_table",
    )(snap, send_up, send_down)


def spread_matrix(tiles):
    spread = np.zeros((3, 3, tiles, 2, 3, tiles, GROUP, 2), np.float32)
    for tile in range(tiles):
        for comp in range(3):
            for half, pair, in_comp in ((0, 0, 0), (0, 1, 1), (1, 0, 2)):
                spread[comp, in_comp, tile, half, comp, tile, :, pair] = 1.0
    return jnp.asarray(spread.reshape(tiles * 9, 6 * tiles * GROUP * 2), BF16)


def spread_kernel(tile_ref, spread_ref, out_ref):
    depth = out_ref.shape[2]
    turned = tile_ref[...].astype(F32).T.astype(BF16)
    node = lax.broadcasted_iota(jnp.int32, (GROUP, depth), 0)
    slot = (lax.broadcasted_iota(jnp.int32, (GROUP, depth), 1) // 2) % GROUP
    own = node == slot
    for pair in range(3):
        both = [
            jnp.dot(turned, spread_ref[:, (2 * pair + one) * depth : (2 * pair + one + 1) * depth], preferred_element_type=F32)
            for one in range(2)
        ]
        for group in range(out_ref.shape[0]):
            kept = [jnp.where(own, part[group * GROUP : (group + 1) * GROUP], 0.0) for part in both]
            out_ref[group, 16 * pair : 16 * (pair + 1), :] = jnp.concatenate(kept, axis=0).astype(BF16)


def spread_tiles(mass_tiles):
    tiles, _, _, node_count = mass_tiles.shape
    depth = tiles * GROUP * 2
    step = LANES
    spread = spread_matrix(tiles)
    return pl.pallas_call(
        spread_kernel,
        grid=(node_count // step,),
        in_specs=[
            pl.BlockSpec((tiles * 9, step), lambda i: (0, i)),
            pl.BlockSpec(spread.shape, lambda i: (0, 0)),
        ],
        out_specs=pl.BlockSpec((step // GROUP, 48, depth), lambda i: (i, 0, 0)),
        out_shape=jax.ShapeDtypeStruct((node_count // GROUP, 48, depth), BF16),
        cost_estimate=pl.CostEstimate(flops=2 * node_count * tiles * 9 * 6 * depth, bytes_accessed=node_count * 6 * depth * 2, transcendentals=0),
        name="spread_tiles",
    )(jnp.transpose(mass_tiles, (1, 2, 0, 3)).reshape(tiles * 9, node_count), spread)


def mass_kernel(slot_hbm, table_hbm, lower_hbm, upper_hbm, left_ref, out_ref, slots0, slots1, table_ref, turn_ref, sem, fill_sem):
    step, steps = pl.program_id(0), pl.num_programs(0)
    others = slot_hbm.shape[0]
    nodes, halo = table_hbm.shape[0], lower_hbm.shape[0]
    low_half = lax.broadcasted_iota(jnp.int32, (GROUP, LANES), 1) < HALF
    slot_refs = (slots0, slots1)

    def fetch(block, part):
        source = slot_hbm.at[:, pl.ds(pl.multiple_of(block * LANES, LANES), LANES)]
        return pltpu.make_async_copy(source, slot_refs[part], sem.at[part])

    @pl.when(step == 0)
    def _():
        fetch(0, 0).start()
        fetch(1, 1).start()
        fills = [
            pltpu.make_async_copy(table_hbm, table_ref.at[pl.ds(0, nodes)], fill_sem.at[0]),
            pltpu.make_async_copy(lower_hbm, table_ref.at[pl.ds(nodes, halo)], fill_sem.at[1]),
            pltpu.make_async_copy(upper_hbm, table_ref.at[pl.ds(nodes + halo, halo)], fill_sem.at[2]),
        ]
        for fill in fills:
            fill.start()
        for fill in fills:
            fill.wait()

    for part in range(2):
        block = 2 * step + part
        fetch(block, part).wait()
        for group in range(LANES // GROUP):
            first = block * LANES + group * GROUP
            rows = [table_ref[pl.ds(first, GROUP)].reshape(2 * GROUP, LANES)]
            for tile in range(others):
                found = [table_ref[slot_refs[part][tile, group * GROUP + node]] for node in range(GROUP)]
                rows.append(jnp.stack(found).reshape(2 * GROUP, LANES))
            sums = jnp.dot(left_ref[part * (LANES // GROUP) + group], jnp.concatenate(rows, axis=0), preferred_element_type=F32)
            for comp in range(3):
                low = sums[comp * GROUP : (comp + 1) * GROUP]
                high = sums[(3 + comp) * GROUP : (4 + comp) * GROUP]
                turn_ref[comp, group * GROUP : (group + 1) * GROUP, :] = jnp.where(low_half, low, high)

        @pl.when(step < steps - 1)
        def _():
            fetch(block + 2, part).start()

        for comp in range(3):
            turned = turn_ref[comp].T
            out_ref[comp, :, part * LANES : (part + 1) * LANES] = (turned[:HALF] + turned[HALF:]).astype(BF16)


def apply_mass(table, from_lower, from_upper, left, tile_slot):
    nodes, halo = table.shape[0], from_lower.shape[0]
    others = tile_slot.shape[0]
    any_space = pl.BlockSpec(memory_space=pl.ANY)
    groups = 2 * LANES // GROUP
    return pl.pallas_call(
        mass_kernel,
        grid=(nodes // (2 * LANES),),
        in_specs=[any_space] * 4 + [pl.BlockSpec((groups, 48, left.shape[2]), lambda i: (i, 0, 0))],
        out_specs=pl.BlockSpec((3, HALF, 2 * LANES), lambda i: (0, 0, i)),
        out_shape=jax.ShapeDtypeStruct((3, HALF, nodes), BF16),
        scratch_shapes=[
            pltpu.SMEM((others, LANES), jnp.int32),
            pltpu.SMEM((others, LANES), jnp.int32),
            pltpu.VMEM((nodes + 2 * halo, 2, LANES), BF16),
            pltpu.VMEM((3, LANES, LANES), F32),
            pltpu.SemaphoreType.DMA((2,)),
            pltpu.SemaphoreType.DMA((3,)),
        ],
        cost_estimate=pl.CostEstimate(flops=2 * nodes * 6 * left.shape[2] * LANES, bytes_accessed=left.size * 2, transcendentals=0),
        name="mass_rows",
    )(tile_slot, table, from_lower, from_upper, left)


def summed(value, axis):
    count = lax.axis_size(axis)
    if count & (count - 1):
        return lax.psum(value, axis)
    step = 1
    while step < count:
        value = value + lax.ppermute(value, axis, [(source, source ^ step) for source in range(count)])
        step *= 2
    return value


def in_order(blocks):
    cols, here = len(blocks), lax.axis_index("col")
    if cols == 2:
        first = here == 0
        return jnp.concatenate([jnp.where(first, *blocks), jnp.where(first, *blocks[::-1])], axis=1)
    return jnp.concatenate([lax.dynamic_index_in_dim(jnp.stack(blocks), lax.rem(here - col + cols, cols), 0, False) for col in range(cols)], axis=1)


def body(snapshots, mass_tiles, tile_slot, send_up, send_down):
    snap_count, _, node_count = snapshots.shape
    cols = lax.axis_size("col")
    by_comp = jnp.transpose(snapshots, (1, 0, 2))
    parts = [by_comp] + [
        lax.ppermute(by_comp, "col", [(source, (source + shift) % cols) for source in range(cols)])
        for shift in range(1, cols)
    ]
    left = spread_tiles(mass_tiles)
    pieces = []
    for start in range(0, snap_count, HALF):
        piece = by_comp[:, start : start + HALF]
        size = piece.shape[1]
        if size < HALF:
            piece = jnp.pad(piece, ((0, 0), (0, HALF - size), (0, 0)))
        table, to_upper, to_lower = node_table(piece, send_up, send_down)
        from_lower = shifted(to_upper, "dom", 1)
        from_upper = shifted(to_lower, "dom", -1)
        pieces.append(apply_mass(table, from_lower, from_upper, left, tile_slot)[:, :size])
    mass_rows = pieces[0] if len(pieces) == 1 else jnp.concatenate(pieces, axis=1)
    blocks = [lax.dot_general(mass_rows, part, (((0, 2), (0, 2)), ((), ())), preferred_element_type=F32) for part in parts]
    total = summed(in_order(blocks), "dom") / (3.0 * node_count * lax.axis_size("dom"))
    return jnp.transpose(mass_rows, (1, 0, 2)), total.T


def solution(mesh):
    placed = (P("col", None, "dom"), P(None, None, None, "dom"), P(None, "dom"), P("dom"), P("dom"))
    return jax.shard_map(
        body,
        mesh=mesh,
        in_specs=placed,
        out_specs=(P("col", None, "dom"), P(None, "col")),
        check_vma=False,
    )
```

```python
import functools

import jax
import jax.numpy as jnp
import numpy as np
from jax import lax
from jax.experimental import pallas as pl
from jax.experimental.pallas import tpu as pltpu
from jax.sharding import PartitionSpec as P

LANES = 128
HALF = LANES // 2
GROUP = 8
BF16 = jnp.bfloat16
F32 = jnp.float32


def shifted(value, axis, steps):
    count = lax.axis_size(axis)
    leading, last = (max(0, -steps), min(count, count - steps))
    return lax.ppermute(value, axis, [(source, source + steps) for source in range(leading, last)])


def nt_dot(left, right):
    return lax.dot_general(left, right, (((1,), (1,)), ((), ())), preferred_element_type=F32)


def table_kernel(snap_ref, up_ref, down_ref, table_ref, to_upper_ref, to_lower_ref):
    node_count = snap_ref.shape[2]
    row = lax.broadcasted_iota(jnp.int32, (2 * LANES, 2 * LANES), 0)
    col = lax.broadcasted_iota(jnp.int32, (2 * LANES, 2 * LANES), 1)
    pick = jnp.where(col == (row // 2) + LANES * (row % 2), 1.0, 0.0).astype(BF16)
    empty = jnp.zeros((HALF, LANES), BF16)
    for start in range(0, node_count, LANES):
        comps = [snap_ref[comp, :, start : start + LANES] for comp in range(3)]
        first = jnp.concatenate([comps[0], comps[2]], axis=0)
        second = jnp.concatenate([comps[1], empty], axis=0)
        rows = nt_dot(pick, jnp.concatenate([first, second], axis=1)).astype(BF16)
        table_ref[start : start + LANES] = rows.reshape(LANES, 2, LANES)
    for out_ref, list_ref in ((to_upper_ref, up_ref), (to_lower_ref, down_ref)):
        for entry in range(out_ref.shape[0]):
            out_ref[entry] = table_ref[list_ref[entry]]


def node_table(snap, send_up, send_down):
    node_count = snap.shape[2]
    halo = send_up.shape[0]
    smem = pl.BlockSpec(memory_space=pltpu.SMEM)
    vmem = pl.BlockSpec(memory_space=pltpu.VMEM)
    return pl.pallas_call(
        table_kernel,
        in_specs=[vmem, smem, smem],
        out_specs=[vmem] * 3,
        out_shape=[
            jax.ShapeDtypeStruct((node_count, 2, LANES), BF16),
            jax.ShapeDtypeStruct((halo, 2, LANES), BF16),
            jax.ShapeDtypeStruct((halo, 2, LANES), BF16),
        ],
        name="node_table",
    )(snap, send_up, send_down)


def spread_matrix(tiles):
    spread = np.zeros((3, 3, tiles, 2, 3, tiles, GROUP, 2), np.float32)
    for tile in range(tiles):
        for comp in range(3):
            for half, pair, in_comp in ((0, 0, 0), (0, 1, 1), (1, 0, 2)):
                spread[comp, in_comp, tile, half, comp, tile, :, pair] = 1.0
    return jnp.asarray(spread.reshape(tiles * 9, 6 * tiles * GROUP * 2), BF16)


def spread_kernel(tile_ref, spread_ref, out_ref):
    sides = out_ref.shape[0]
    depth = sides * LANES
    groups = LANES // GROUP
    node = lax.broadcasted_iota(jnp.int32, (GROUP, depth), 0)
    slot = (lax.broadcasted_iota(jnp.int32, (GROUP, depth), 1) // 2) % GROUP
    own = node == slot
    for block in range(tile_ref.shape[1] // LANES):
        turned = tile_ref[:, block * LANES : (block + 1) * LANES].T
        for pair in range(3):
            both = [
                jnp.dot(turned, spread_ref[:, (2 * pair + one) * depth : (2 * pair + one + 1) * depth], preferred_element_type=F32)
                for one in range(2)
            ]
            for group in range(groups):
                kept = [jnp.where(own, part[group * GROUP : (group + 1) * GROUP], 0.0) for part in both]
                rows = jnp.concatenate(kept, axis=0).astype(BF16)
                for side in range(sides):
                    out_ref[side, block * groups + group, 16 * pair : 16 * (pair + 1), :] = rows[:, side * LANES : (side + 1) * LANES]


def spread_tiles(mass_tiles):
    tiles, _, _, node_count = mass_tiles.shape
    depth = tiles * GROUP * 2
    step = min(node_count, 4 * LANES)
    spread = spread_matrix(tiles)
    return pl.pallas_call(
        spread_kernel,
        grid=(node_count // step,),
        in_specs=[
            pl.BlockSpec((tiles * 9, step), lambda i: (0, i)),
            pl.BlockSpec(spread.shape, lambda i: (0, 0)),
        ],
        out_specs=pl.BlockSpec((depth // LANES, step // GROUP, 48, LANES), lambda i: (0, i, 0, 0)),
        out_shape=jax.ShapeDtypeStruct((depth // LANES, node_count // GROUP, 48, LANES), BF16),
        cost_estimate=pl.CostEstimate(flops=2 * node_count * tiles * 9 * 6 * depth, bytes_accessed=node_count * 6 * depth * 2, transcendentals=0),
        name="spread_tiles",
    )(jnp.transpose(mass_tiles, (1, 2, 0, 3)).reshape(tiles * 9, node_count), spread)


def mass_kernel(parts, slot_hbm, table_hbm, lower_hbm, upper_hbm, left_hbm, own_hbm, out_ref, *scratch):
    slot_refs, left_refs, own_refs = (scratch[kind * parts : (kind + 1) * parts] for kind in range(3))
    table_ref, turn_ref, sem, fill_sem = scratch[3 * parts :]
    step, steps = pl.program_id(0), pl.num_programs(0)
    others = slot_hbm.shape[0]
    sides = left_hbm.shape[0]
    nodes, halo = table_hbm.shape[0], lower_hbm.shape[0]
    groups = LANES // GROUP
    low_half = lax.broadcasted_iota(jnp.int32, (GROUP, LANES), 1) < HALF

    def fetches(block, part):
        def window(width):
            return pl.ds(pl.multiple_of(block * width, width), width)

        return (
            pltpu.make_async_copy(slot_hbm.at[:, window(LANES)], slot_refs[part], sem.at[part, 0]),
            pltpu.make_async_copy(left_hbm.at[:, window(groups)], left_refs[part], sem.at[part, 1]),
            pltpu.make_async_copy(own_hbm.at[window(2 * LANES)], own_refs[part], sem.at[part, 2]),
        )

    @pl.when(step == 0)
    def _():
        fills = [
            pltpu.make_async_copy(table_hbm, table_ref.at[pl.ds(0, nodes)], fill_sem.at[0]),
            pltpu.make_async_copy(lower_hbm, table_ref.at[pl.ds(nodes, halo)], fill_sem.at[1]),
            pltpu.make_async_copy(upper_hbm, table_ref.at[pl.ds(nodes + halo, halo)], fill_sem.at[2]),
        ]
        for copy in (*fetches(0, 0), *fills):
            copy.start()
        for part in range(1, parts):
            for copy in fetches(part, part):
                copy.start()
        for fill in fills:
            fill.wait()

    for part in range(parts):
        block = parts * step + part
        for copy in fetches(block, part):
            copy.wait()
        for group in range(groups):
            rows = [own_refs[part][2 * GROUP * group : 2 * GROUP * (group + 1), :]]
            for tile in range(others):
                found = [table_ref[slot_refs[part][tile, group * GROUP + node]] for node in range(GROUP)]
                rows.append(jnp.stack(found).reshape(2 * GROUP, LANES))
            left = jnp.concatenate([left_refs[part][side, group] for side in range(sides)], axis=1)
            sums = jnp.dot(left, jnp.concatenate(rows, axis=0), preferred_element_type=F32)
            for comp in range(3):
                low = sums[comp * GROUP : (comp + 1) * GROUP]
                high = sums[(3 + comp) * GROUP : (4 + comp) * GROUP]
                turn_ref[comp, group * GROUP : (group + 1) * GROUP, :] = jnp.where(low_half, low, high)

        @pl.when(step < steps - 1)
        def _():
            for copy in fetches(block + parts, part):
                copy.start()

        for comp in range(3):
            turned = turn_ref[comp].T
            out_ref[comp, :, part * LANES : (part + 1) * LANES] = (turned[:HALF] + turned[HALF:]).astype(BF16)


def apply_mass(table, from_lower, from_upper, left, tile_slot):
    nodes, halo = table.shape[0], from_lower.shape[0]
    others = tile_slot.shape[0]
    sides = left.shape[0]
    blocks = nodes // LANES
    parts = next(count for count in (4, 2, 1) if blocks % count == 0)
    any_space = pl.BlockSpec(memory_space=pl.ANY)
    return pl.pallas_call(
        functools.partial(mass_kernel, parts),
        grid=(blocks // parts,),
        in_specs=[any_space] * 6,
        out_specs=pl.BlockSpec((3, HALF, parts * LANES), lambda i: (0, 0, i)),
        out_shape=jax.ShapeDtypeStruct((3, HALF, nodes), BF16),
        scratch_shapes=[pltpu.SMEM((others, LANES), jnp.int32)] * parts
        + [pltpu.VMEM((sides, LANES // GROUP, 48, LANES), BF16)] * parts
        + [pltpu.VMEM((2 * LANES, LANES), BF16)] * parts
        + [
            pltpu.VMEM((nodes + 2 * halo, 2, LANES), BF16),
            pltpu.VMEM((3, LANES, LANES), F32),
            pltpu.SemaphoreType.DMA((parts, 3)),
            pltpu.SemaphoreType.DMA((3,)),
        ],
        cost_estimate=pl.CostEstimate(flops=2 * nodes * 6 * sides * LANES * LANES, bytes_accessed=left.size * 2, transcendentals=0),
        name="mass_rows",
    )(tile_slot, table, from_lower, from_upper, left, table.reshape(2 * nodes, LANES))


def summed(value, axis):
    count = lax.axis_size(axis)
    if count & (count - 1):
        return lax.psum(value, axis)
    step = 1
    while step < count:
        value = value + lax.ppermute(value, axis, [(source, source ^ step) for source in range(count)])
        step *= 2
    return value


def in_order(blocks):
    cols, here = len(blocks), lax.axis_index("col")
    if cols == 2:
        first = here == 0
        return jnp.concatenate([jnp.where(first, *blocks), jnp.where(first, *blocks[::-1])], axis=1)
    return jnp.concatenate([lax.dynamic_index_in_dim(jnp.stack(blocks), lax.rem(here - col + cols, cols), 0, False) for col in range(cols)], axis=1)


def body(snapshots, mass_tiles, tile_slot, send_up, send_down):
    snap_count, _, node_count = snapshots.shape
    cols = lax.axis_size("col")
    by_comp = jnp.transpose(snapshots, (1, 0, 2))
    parts = [by_comp] + [
        lax.ppermute(by_comp, "col", [(source, (source + shift) % cols) for source in range(cols)])
        for shift in range(1, cols)
    ]
    left = spread_tiles(mass_tiles)
    pieces = []
    for start in range(0, snap_count, HALF):
        piece = by_comp[:, start : start + HALF]
        size = piece.shape[1]
        if size < HALF:
            piece = jnp.pad(piece, ((0, 0), (0, HALF - size), (0, 0)))
        table, to_upper, to_lower = node_table(piece, send_up, send_down)
        from_lower = shifted(to_upper, "dom", 1)
        from_upper = shifted(to_lower, "dom", -1)
        pieces.append(apply_mass(table, from_lower, from_upper, left, tile_slot)[:, :size])
    mass_rows = pieces[0] if len(pieces) == 1 else jnp.concatenate(pieces, axis=1)
    blocks = [lax.dot_general(mass_rows, part, (((0, 2), (0, 2)), ((), ())), preferred_element_type=F32) for part in parts]
    total = summed(in_order(blocks), "dom") / (3.0 * node_count * lax.axis_size("dom"))
    return jnp.transpose(mass_rows, (1, 0, 2)), total.T


def solution(mesh):
    placed = (P("col", None, "dom"), P(None, None, None, "dom"), P(None, "dom"), P("dom"), P("dom"))
    return jax.shard_map(
        body,
        mesh=mesh,
        in_specs=placed,
        out_specs=(P("col", None, "dom"), P(None, "col")),
        check_vma=False,
    )
```

```python
import functools

import jax
import jax.numpy as jnp
import numpy as np
from jax import lax
from jax.experimental import pallas as pl
from jax.experimental.pallas import tpu as pltpu
from jax.sharding import PartitionSpec as P

LANES = 128
HALF = LANES // 2
GROUP = 8
VMEM_BYTES = 20 * 2**20
BF16 = jnp.bfloat16
F32 = jnp.float32


def swap(value, axis, first):
    count = lax.axis_size(axis)
    pairs = [(low, low + 1) for low in range(first, count - 1, 2)]
    return lax.ppermute(value, axis, pairs + [(high, low) for low, high in pairs])


def nt_dot(left, right):
    return lax.dot_general(left, right, (((1,), (1,)), ((), ())), preferred_element_type=F32)


def table_kernel(snap_ref, near_ref, far_ref, table_ref, to_near_ref, to_far_ref):
    node_count = snap_ref.shape[2]
    row = lax.broadcasted_iota(jnp.int32, (2 * LANES, 2 * LANES), 0)
    col = lax.broadcasted_iota(jnp.int32, (2 * LANES, 2 * LANES), 1)
    pick = jnp.where(col == (row // 2) + LANES * (row % 2), 1.0, 0.0).astype(BF16)
    empty = jnp.zeros((HALF, LANES), BF16)
    for start in range(0, node_count, LANES):
        comps = [snap_ref[comp, :, start : start + LANES] for comp in range(3)]
        first = jnp.concatenate([comps[0], comps[2]], axis=0)
        second = jnp.concatenate([comps[1], empty], axis=0)
        rows = nt_dot(pick, jnp.concatenate([first, second], axis=1)).astype(BF16)
        table_ref[start : start + LANES] = rows.reshape(LANES, 2, LANES)
    for out_ref, list_ref in ((to_near_ref, near_ref), (to_far_ref, far_ref)):
        for entry in range(out_ref.shape[0]):
            out_ref[entry] = table_ref[list_ref[entry]]


def node_table(snap, near_list, far_list):
    node_count = snap.shape[2]
    halo = near_list.shape[0]
    smem = pl.BlockSpec(memory_space=pltpu.SMEM)
    vmem = pl.BlockSpec(memory_space=pltpu.VMEM)
    return pl.pallas_call(
        table_kernel,
        in_specs=[vmem, smem, smem],
        out_specs=[vmem] * 3,
        out_shape=[
            jax.ShapeDtypeStruct((node_count, 2, LANES), BF16),
            jax.ShapeDtypeStruct((halo, 2, LANES), BF16),
            jax.ShapeDtypeStruct((halo, 2, LANES), BF16),
        ],
        compiler_params=pltpu.CompilerParams(vmem_limit_bytes=VMEM_BYTES),
        name="node_table",
    )(snap, near_list, far_list)


def spread_matrix(tiles):
    spread = np.zeros((3, 3, tiles, 2, 3, tiles, GROUP, 2), np.float32)
    for tile in range(tiles):
        for comp in range(3):
            for half, pair, in_comp in ((0, 0, 0), (0, 1, 1), (1, 0, 2)):
                spread[comp, in_comp, tile, half, comp, tile, :, pair] = 1.0
    return jnp.asarray(spread.reshape(tiles * 9, 6 * tiles * GROUP * 2), BF16)


def spread_kernel(tile_ref, spread_ref, out_ref):
    sides = out_ref.shape[0]
    depth = sides * LANES
    groups = LANES // GROUP
    node = lax.broadcasted_iota(jnp.int32, (GROUP, depth), 0)
    slot = (lax.broadcasted_iota(jnp.int32, (GROUP, depth), 1) // 2) % GROUP
    own = node == slot
    for block in range(tile_ref.shape[1] // LANES):
        turned = tile_ref[:, block * LANES : (block + 1) * LANES].T
        for pair in range(3):
            both = [
                jnp.dot(turned, spread_ref[:, (2 * pair + one) * depth : (2 * pair + one + 1) * depth], preferred_element_type=F32)
                for one in range(2)
            ]
            for group in range(groups):
                kept = [jnp.where(own, part[group * GROUP : (group + 1) * GROUP], 0.0) for part in both]
                rows = jnp.concatenate(kept, axis=0).astype(BF16)
                for side in range(sides):
                    out_ref[side, block * groups + group, 16 * pair : 16 * (pair + 1), :] = rows[:, side * LANES : (side + 1) * LANES]


def spread_tiles(mass_tiles):
    tiles, _, _, node_count = mass_tiles.shape
    depth = tiles * GROUP * 2
    step = min(node_count, 4 * LANES)
    spread = spread_matrix(tiles)
    return pl.pallas_call(
        spread_kernel,
        grid=(node_count // step,),
        in_specs=[
            pl.BlockSpec((tiles * 9, step), lambda i: (0, i)),
            pl.BlockSpec(spread.shape, lambda i: (0, 0)),
        ],
        out_specs=pl.BlockSpec((depth // LANES, step // GROUP, 48, LANES), lambda i: (0, i, 0, 0)),
        out_shape=jax.ShapeDtypeStruct((depth // LANES, node_count // GROUP, 48, LANES), BF16),
        cost_estimate=pl.CostEstimate(flops=2 * node_count * tiles * 9 * 6 * depth, bytes_accessed=node_count * 6 * depth * 2, transcendentals=0),
        compiler_params=pltpu.CompilerParams(vmem_limit_bytes=VMEM_BYTES),
        name="spread_tiles",
    )(jnp.transpose(mass_tiles, (1, 2, 0, 3)).reshape(tiles * 9, node_count), spread)


def mass_kernel(parts, slot_hbm, table_hbm, near_in, far_in, left_hbm, own_hbm, out_ref, again_ref, *scratch):
    slot_refs, left_refs, own_refs = (scratch[kind * parts : (kind + 1) * parts] for kind in range(3))
    table_ref, turn_ref, sem, fill_sem = scratch[3 * parts :]
    step, steps = pl.program_id(0), pl.num_programs(0)
    others = slot_hbm.shape[0]
    sides = left_hbm.shape[0]
    nodes, halo = table_hbm.shape[0], near_in.shape[0]
    groups = LANES // GROUP
    low_half = lax.broadcasted_iota(jnp.int32, (GROUP, LANES), 1) < HALF

    def fetches(block, part):
        def window(width):
            return pl.ds(pl.multiple_of(block * width, width), width)

        return (
            pltpu.make_async_copy(slot_hbm.at[:, window(LANES)], slot_refs[part], sem.at[part, 0]),
            pltpu.make_async_copy(left_hbm.at[:, window(groups)], left_refs[part], sem.at[part, 1]),
            pltpu.make_async_copy(own_hbm.at[window(2 * LANES)], own_refs[part], sem.at[part, 2]),
        )

    @pl.when(step == 0)
    def _():
        odd = lax.rem(lax.axis_index("dom"), 2)
        fills = [
            pltpu.make_async_copy(table_hbm, table_ref.at[pl.ds(0, nodes)], fill_sem.at[0]),
            pltpu.make_async_copy(near_in, table_ref.at[pl.ds(nodes + (1 - odd) * halo, halo)], fill_sem.at[1]),
            pltpu.make_async_copy(far_in, table_ref.at[pl.ds(nodes + odd * halo, halo)], fill_sem.at[2]),
        ]
        for copy in (*fetches(0, 0), *fills):
            copy.start()
        for part in range(1, parts):
            for copy in fetches(part, part):
                copy.start()
        for fill in fills:
            fill.wait()

    for part in range(parts):
        block = parts * step + part
        for copy in fetches(block, part):
            copy.wait()
        for group in range(groups):
            rows = [own_refs[part][2 * GROUP * group : 2 * GROUP * (group + 1), :]]
            for tile in range(others):
                found = [table_ref[slot_refs[part][tile, group * GROUP + node]] for node in range(GROUP)]
                rows.append(jnp.stack(found).reshape(2 * GROUP, LANES))
            left = jnp.concatenate([left_refs[part][side, group] for side in range(sides)], axis=1)
            sums = jnp.dot(left, jnp.concatenate(rows, axis=0), preferred_element_type=F32)
            for comp in range(3):
                low = sums[comp * GROUP : (comp + 1) * GROUP]
                high = sums[(3 + comp) * GROUP : (4 + comp) * GROUP]
                turn_ref[comp, group * GROUP : (group + 1) * GROUP, :] = jnp.where(low_half, low, high)

        @pl.when(step < steps - 1)
        def _():
            for copy in fetches(block + parts, part):
                copy.start()

        for comp in range(3):
            turned = turn_ref[comp].T
            rounded = (turned[:HALF] + turned[HALF:]).astype(BF16)
            out_ref[comp, :, part * LANES : (part + 1) * LANES] = rounded
            again_ref[comp, :, part * LANES : (part + 1) * LANES] = rounded


def apply_mass(table, from_near, from_far, left, tile_slot):
    nodes, halo = table.shape[0], from_near.shape[0]
    others = tile_slot.shape[0]
    sides = left.shape[0]
    blocks = nodes // LANES
    parts = next(count for count in (4, 2, 1) if blocks % count == 0)
    any_space = pl.BlockSpec(memory_space=pl.ANY)
    return pl.pallas_call(
        functools.partial(mass_kernel, parts),
        grid=(blocks // parts,),
        in_specs=[any_space] * 2 + [pl.BlockSpec(memory_space=pltpu.VMEM)] * 2 + [any_space] * 2,
        out_specs=[pl.BlockSpec((3, HALF, parts * LANES), lambda i: (0, 0, i))] * 2,
        out_shape=[jax.ShapeDtypeStruct((3, HALF, nodes), BF16)] * 2,
        scratch_shapes=[pltpu.SMEM((others, LANES), jnp.int32)] * parts
        + [pltpu.VMEM((sides, LANES // GROUP, 48, LANES), BF16)] * parts
        + [pltpu.VMEM((2 * LANES, LANES), BF16)] * parts
        + [
            pltpu.VMEM((nodes + 2 * halo, 2, LANES), BF16),
            pltpu.VMEM((3, LANES, LANES), F32),
            pltpu.SemaphoreType.DMA((parts, 3)),
            pltpu.SemaphoreType.DMA((3,)),
        ],
        cost_estimate=pl.CostEstimate(flops=2 * nodes * 6 * sides * LANES * LANES, bytes_accessed=left.size * 2, transcendentals=0),
        compiler_params=pltpu.CompilerParams(vmem_limit_bytes=VMEM_BYTES),
        name="mass_rows",
    )(tile_slot, table, from_near, from_far, left, table.reshape(2 * nodes, LANES))


def summed(value, axis):
    count = lax.axis_size(axis)
    if count & (count - 1):
        return lax.psum(value, axis)
    step = 1
    while step < count:
        value = value + lax.ppermute(value, axis, [(source, source ^ step) for source in range(count)])
        step *= 2
    return value


def in_order(blocks):
    cols, here = len(blocks), lax.axis_index("col")
    if cols == 2:
        first = here == 0
        return jnp.concatenate([jnp.where(first, *blocks), jnp.where(first, *blocks[::-1])], axis=1)
    return jnp.concatenate([lax.dynamic_index_in_dim(jnp.stack(blocks), lax.rem(here - col + cols, cols), 0, False) for col in range(cols)], axis=1)


def body(snapshots, mass_tiles, tile_slot, send_up, send_down):
    snap_count, _, node_count = snapshots.shape
    cols = lax.axis_size("col")
    by_comp = jnp.transpose(snapshots, (1, 0, 2))
    parts = [by_comp] + [
        lax.ppermute(by_comp, "col", [(source, (source + shift) % cols) for source in range(cols)])
        for shift in range(1, cols)
    ]
    left = spread_tiles(mass_tiles)
    even = lax.rem(lax.axis_index("dom"), 2) == 0
    near_list, far_list = jnp.where(even, send_up, send_down), jnp.where(even, send_down, send_up)
    pieces = []
    for start in range(0, snap_count, HALF):
        piece = by_comp[:, start : start + HALF]
        size = piece.shape[1]
        if size < HALF:
            piece = jnp.pad(piece, ((0, 0), (0, HALF - size), (0, 0)))
        table, to_near, to_far = node_table(piece, near_list, far_list)
        both = apply_mass(table, swap(to_near, "dom", 0), swap(to_far, "dom", 1), left, tile_slot)
        pieces.append([rows[:, :size] for rows in both])
    mass_rows, again = pieces[0] if len(pieces) == 1 else [jnp.concatenate(rows, axis=1) for rows in zip(*pieces)]
    blocks = [lax.dot_general(again, part, (((0, 2), (0, 2)), ((), ())), preferred_element_type=F32) for part in parts]
    total = summed(in_order(blocks), "dom") / (3.0 * node_count * lax.axis_size("dom"))
    return jnp.transpose(mass_rows, (1, 0, 2)), total.T


def solution(mesh):
    placed = (P("col", None, "dom"), P(None, None, None, "dom"), P(None, "dom"), P("dom"), P("dom"))
    return jax.shard_map(
        body,
        mesh=mesh,
        in_specs=placed,
        out_specs=(P("col", None, "dom"), P(None, "col")),
        check_vma=False,
    )
```

```python
import functools

import jax
import jax.numpy as jnp
from jax import lax
from jax.experimental import pallas as pl
from jax.experimental.pallas import tpu as pltpu
from jax.sharding import PartitionSpec as P

LANES = 128
HALF = LANES // 2
GROUP = 8
VMEM_BYTES = 20 * 2**20
BF16 = jnp.bfloat16
F32 = jnp.float32


def swap(value, axis, first):
    count = lax.axis_size(axis)
    pairs = [(low, low + 1) for low in range(first, count - 1, 2)]
    return lax.ppermute(value, axis, pairs + [(high, low) for low, high in pairs])


def nt_dot(left, right):
    return lax.dot_general(left, right, (((1,), (1,)), ((), ())), preferred_element_type=F32)


def table_kernel(snap_hbm, up_ref, down_ref, table_ref, to_near_ref, to_far_ref, snap_ref, sem):
    chunks = snap_ref.shape[0]
    width = snap_ref.shape[3]
    copies = [
        pltpu.make_async_copy(snap_hbm.at[:, :, pl.ds(chunk * width, width)], snap_ref.at[chunk], sem.at[chunk])
        for chunk in range(chunks)
    ]
    for copy in copies:
        copy.start()
    row = lax.broadcasted_iota(jnp.int32, (2 * LANES, 2 * LANES), 0)
    col = lax.broadcasted_iota(jnp.int32, (2 * LANES, 2 * LANES), 1)
    pick = jnp.where(col == (row // 2) + LANES * (row % 2), 1.0, 0.0).astype(BF16)
    empty = jnp.zeros((HALF, LANES), BF16)
    for chunk in range(chunks):
        copies[chunk].wait()
        for start in range(0, width, LANES):
            comps = [snap_ref[chunk, comp, :, start : start + LANES] for comp in range(3)]
            first = jnp.concatenate([comps[0], comps[2]], axis=0)
            second = jnp.concatenate([comps[1], empty], axis=0)
            rows = nt_dot(pick, jnp.concatenate([first, second], axis=1)).astype(BF16)
            table_ref[chunk * width + start : chunk * width + start + LANES] = rows.reshape(LANES, 2, LANES)

    def fill(near_list, far_list):
        for out_ref, list_ref in ((to_near_ref, near_list), (to_far_ref, far_list)):
            for entry in range(out_ref.shape[0]):
                out_ref[entry] = table_ref[list_ref[entry]]

    odd = lax.rem(lax.axis_index("dom"), 2)

    @pl.when(odd == 0)
    def _():
        fill(up_ref, down_ref)

    @pl.when(odd == 1)
    def _():
        fill(down_ref, up_ref)


def node_table(snap, send_up, send_down):
    node_count = snap.shape[2]
    halo = send_up.shape[0]
    smem = pl.BlockSpec(memory_space=pltpu.SMEM)
    vmem = pl.BlockSpec(memory_space=pltpu.VMEM)
    chunks = 4 if node_count % (4 * LANES) == 0 else 1
    return pl.pallas_call(
        table_kernel,
        in_specs=[pl.BlockSpec(memory_space=pltpu.HBM), smem, smem],
        out_specs=[vmem] * 3,
        out_shape=[
            jax.ShapeDtypeStruct((node_count, 2, LANES), BF16),
            jax.ShapeDtypeStruct((halo, 2, LANES), BF16),
            jax.ShapeDtypeStruct((halo, 2, LANES), BF16),
        ],
        scratch_shapes=[pltpu.VMEM((chunks, 3, HALF, node_count // chunks), BF16), pltpu.SemaphoreType.DMA((chunks,))],
        compiler_params=pltpu.CompilerParams(vmem_limit_bytes=VMEM_BYTES),
        name="node_table",
    )(*(pltpu.with_memory_space_constraint(operand, pltpu.HBM) for operand in (snap, send_up, send_down)))


def spread_kernel(tile_hbm, out_ref, tile_ref, sem):
    sides = out_ref.shape[0]
    depth = sides * LANES
    groups = LANES // GROUP
    chunks, height, width = tile_ref.shape
    tiles = height // 9
    copies = [
        pltpu.make_async_copy(tile_hbm.at[:, pl.ds(chunk * width, width)], tile_ref.at[chunk], sem.at[chunk])
        for chunk in range(chunks)
    ]
    for copy in copies:
        copy.start()
    row = lax.broadcasted_iota(jnp.int32, (height, depth), 0)
    col = lax.broadcasted_iota(jnp.int32, (height, depth), 1)
    same_tile = row % tiles == col // (2 * GROUP)
    spreads = []
    for half in range(2):
        in_comp = col % 2 if half == 0 else jnp.where(col % 2 == 0, 2, -1)
        for comp in range(3):
            kept = same_tile & (row // tiles == 3 * comp + in_comp) & (in_comp >= 0)
            spreads.append(jnp.where(kept, 1.0, 0.0).astype(BF16))
    node = lax.broadcasted_iota(jnp.int32, (GROUP, depth), 0)
    slot = (lax.broadcasted_iota(jnp.int32, (GROUP, depth), 1) // 2) % GROUP
    own = node == slot
    for chunk in range(chunks):
        copies[chunk].wait()
        for block in range(width // LANES):
            turned = tile_ref[chunk, :, block * LANES : (block + 1) * LANES].T
            first = (chunk * width // LANES + block) * groups
            for pair in range(3):
                both = [jnp.dot(turned, spreads[2 * pair + one], preferred_element_type=F32) for one in range(2)]
                for group in range(groups):
                    kept = [jnp.where(own, part[group * GROUP : (group + 1) * GROUP], 0.0) for part in both]
                    rows = jnp.concatenate(kept, axis=0).astype(BF16)
                    for side in range(sides):
                        out_ref[side, first + group, 16 * pair : 16 * (pair + 1), :] = rows[:, side * LANES : (side + 1) * LANES]


def spread_tiles(mass_tiles):
    tiles, _, _, node_count = mass_tiles.shape
    sides = tiles * GROUP * 2 // LANES
    chunks = 4 if node_count % (4 * LANES) == 0 else 1
    return pl.pallas_call(
        spread_kernel,
        in_specs=[pl.BlockSpec(memory_space=pltpu.HBM)],
        out_specs=pl.BlockSpec(memory_space=pltpu.VMEM),
        out_shape=jax.ShapeDtypeStruct((sides, node_count // GROUP, 48, LANES), BF16),
        scratch_shapes=[pltpu.VMEM((chunks, tiles * 9, node_count // chunks), BF16), pltpu.SemaphoreType.DMA((chunks,))],
        compiler_params=pltpu.CompilerParams(vmem_limit_bytes=VMEM_BYTES),
        cost_estimate=pl.CostEstimate(flops=2 * node_count * tiles * 9 * 6 * sides * LANES, bytes_accessed=node_count * 6 * sides * LANES * 2, transcendentals=0),
        name="spread_tiles",
    )(pltpu.with_memory_space_constraint(jnp.transpose(mass_tiles, (1, 2, 0, 3)).reshape(tiles * 9, node_count), pltpu.HBM))


def mass_kernel(parts, slot_hbm, table_hbm, near_in, far_in, left_ref, own_ref, out_ref, again_ref, *scratch):
    slot_refs = scratch[:parts]
    table_ref, turn_ref, sem, fill_sem = scratch[parts:]
    step, steps = pl.program_id(0), pl.num_programs(0)
    others = slot_hbm.shape[0]
    sides = left_ref.shape[0]
    nodes, halo = table_hbm.shape[0], near_in.shape[0]
    groups = LANES // GROUP
    low_half = lax.broadcasted_iota(jnp.int32, (GROUP, LANES), 1) < HALF

    def fetch(block, part):
        source = slot_hbm.at[:, pl.ds(pl.multiple_of(block * LANES, LANES), LANES)]
        return pltpu.make_async_copy(source, slot_refs[part], sem.at[part])

    @pl.when(step == 0)
    def _():
        odd = lax.rem(lax.axis_index("dom"), 2)
        fills = [
            pltpu.make_async_copy(table_hbm, table_ref.at[pl.ds(0, nodes)], fill_sem.at[0]),
            pltpu.make_async_copy(near_in, table_ref.at[pl.ds(nodes + (1 - odd) * halo, halo)], fill_sem.at[1]),
            pltpu.make_async_copy(far_in, table_ref.at[pl.ds(nodes + odd * halo, halo)], fill_sem.at[2]),
        ]
        for copy in (fetch(0, 0), *fills, *(fetch(part, part) for part in range(1, parts))):
            copy.start()
        for fill in fills:
            fill.wait()

    for part in range(parts):
        block = parts * step + part
        fetch(block, part).wait()
        for group in range(groups):
            rows = [own_ref[pl.ds(pl.multiple_of((block * groups + group) * 2 * GROUP, 2 * GROUP), 2 * GROUP), :]]
            for tile in range(others):
                found = [table_ref[slot_refs[part][tile, group * GROUP + node]] for node in range(GROUP)]
                rows.append(jnp.stack(found).reshape(2 * GROUP, LANES))
            left = jnp.concatenate([left_ref[side, block * groups + group] for side in range(sides)], axis=1)
            sums = jnp.dot(left, jnp.concatenate(rows, axis=0), preferred_element_type=F32)
            for comp in range(3):
                low = sums[comp * GROUP : (comp + 1) * GROUP]
                high = sums[(3 + comp) * GROUP : (4 + comp) * GROUP]
                turn_ref[comp, group * GROUP : (group + 1) * GROUP, :] = jnp.where(low_half, low, high)

        @pl.when(step < steps - 1)
        def _():
            fetch(block + parts, part).start()

        for comp in range(3):
            turned = turn_ref[comp].T
            rounded = (turned[:HALF] + turned[HALF:]).astype(BF16)
            out_ref[comp, :, part * LANES : (part + 1) * LANES] = rounded
            again_ref[comp, :, part * LANES : (part + 1) * LANES] = rounded


def apply_mass(table, from_near, from_far, left, tile_slot):
    nodes, halo = table.shape[0], from_near.shape[0]
    others = tile_slot.shape[0]
    sides = left.shape[0]
    blocks = nodes // LANES
    parts = next(count for count in (4, 2, 1) if blocks % count == 0)
    any_space = pl.BlockSpec(memory_space=pl.ANY)
    return pl.pallas_call(
        functools.partial(mass_kernel, parts),
        grid=(blocks // parts,),
        in_specs=[any_space] * 2 + [pl.BlockSpec(memory_space=pltpu.VMEM)] * 4,
        out_specs=[pl.BlockSpec((3, HALF, parts * LANES), lambda i: (0, 0, i))] * 2,
        out_shape=[jax.ShapeDtypeStruct((3, HALF, nodes), BF16)] * 2,
        scratch_shapes=[pltpu.SMEM((others, LANES), jnp.int32)] * parts
        + [
            pltpu.VMEM((nodes + 2 * halo, 2, LANES), BF16),
            pltpu.VMEM((3, LANES, LANES), F32),
            pltpu.SemaphoreType.DMA((parts,)),
            pltpu.SemaphoreType.DMA((3,)),
        ],
        cost_estimate=pl.CostEstimate(flops=2 * nodes * 6 * sides * LANES * LANES, bytes_accessed=left.size * 2, transcendentals=0),
        compiler_params=pltpu.CompilerParams(vmem_limit_bytes=VMEM_BYTES),
        name="mass_rows",
    )(tile_slot, table, from_near, from_far, left, table.reshape(2 * nodes, LANES))


def summed(value, axis):
    count = lax.axis_size(axis)
    if count & (count - 1):
        return lax.psum(value, axis)
    step = 1
    while step < count:
        value = value + lax.ppermute(value, axis, [(source, source ^ step) for source in range(count)])
        step *= 2
    return value


def in_order(blocks):
    cols, here = len(blocks), lax.axis_index("col")
    if cols == 2:
        first = here == 0
        return jnp.concatenate([jnp.where(first, *blocks), jnp.where(first, *blocks[::-1])], axis=1)
    return jnp.concatenate([lax.dynamic_index_in_dim(jnp.stack(blocks), lax.rem(here - col + cols, cols), 0, False) for col in range(cols)], axis=1)


def body(snapshots, mass_tiles, tile_slot, send_up, send_down):
    snap_count, _, node_count = snapshots.shape
    cols = lax.axis_size("col")
    by_comp = jnp.transpose(snapshots, (1, 0, 2))
    parts = [by_comp] + [
        lax.ppermute(by_comp, "col", [(source, (source + shift) % cols) for source in range(cols)])
        for shift in range(1, cols)
    ]
    left = spread_tiles(mass_tiles)
    pieces = []
    for start in range(0, snap_count, HALF):
        piece = by_comp[:, start : start + HALF]
        size = piece.shape[1]
        if size < HALF:
            piece = jnp.pad(piece, ((0, 0), (0, HALF - size), (0, 0)))
        table, to_near, to_far = node_table(piece, send_up, send_down)
        both = apply_mass(table, swap(to_near, "dom", 0), swap(to_far, "dom", 1), left, tile_slot)
        pieces.append([rows[:, :size] for rows in both])
    mass_rows, again = pieces[0] if len(pieces) == 1 else [jnp.concatenate(rows, axis=1) for rows in zip(*pieces)]
    blocks = [lax.dot_general(again, part, (((0, 2), (0, 2)), ((), ())), preferred_element_type=F32) for part in parts]
    total = summed(in_order(blocks), "dom") / (3.0 * node_count * lax.axis_size("dom"))
    return jnp.transpose(mass_rows, (1, 0, 2)), total.T


def solution(mesh):
    placed = (P("col", None, "dom"), P(None, None, None, "dom"), P(None, "dom"), P("dom"), P("dom"))
    return jax.shard_map(
        body,
        mesh=mesh,
        in_specs=placed,
        out_specs=(P("col", None, "dom"), P(None, "col")),
        check_vma=False,
    )
```

```python
import functools

import jax
import jax.numpy as jnp
from jax import lax
from jax.experimental import pallas as pl
from jax.experimental.pallas import tpu as pltpu
from jax.sharding import PartitionSpec as P

LANES = 128
HALF = LANES // 2
GROUP = 8
VMEM_BYTES = 20 * 2**20
BF16 = jnp.bfloat16
F32 = jnp.float32


def swap(value, axis, first):
    count = lax.axis_size(axis)
    pairs = [(low, low + 1) for low in range(first, count - 1, 2)]
    return lax.ppermute(value, axis, pairs + [(high, low) for low, high in pairs])


def nt_dot(left, right):
    return lax.dot_general(left, right, (((1,), (1,)), ((), ())), preferred_element_type=F32)


def table_kernel(snap_hbm, up_ref, down_ref, table_ref, to_near_ref, to_far_ref, snap_ref, sem):
    chunks = snap_ref.shape[0]
    width = snap_ref.shape[3]
    copies = [
        pltpu.make_async_copy(snap_hbm.at[:, :, pl.ds(chunk * width, width)], snap_ref.at[chunk], sem.at[chunk])
        for chunk in range(chunks)
    ]
    for copy in copies:
        copy.start()
    row = lax.broadcasted_iota(jnp.int32, (2 * LANES, 2 * LANES), 0)
    col = lax.broadcasted_iota(jnp.int32, (2 * LANES, 2 * LANES), 1)
    pick = jnp.where(col == (row // 2) + LANES * (row % 2), 1.0, 0.0).astype(BF16)
    empty = jnp.zeros((HALF, LANES), BF16)
    for chunk in range(chunks):
        copies[chunk].wait()
        for start in range(0, width, LANES):
            comps = [snap_ref[chunk, comp, :, start : start + LANES] for comp in range(3)]
            first = jnp.concatenate([comps[0], comps[2]], axis=0)
            second = jnp.concatenate([comps[1], empty], axis=0)
            rows = nt_dot(pick, jnp.concatenate([first, second], axis=1)).astype(BF16)
            table_ref[chunk * width + start : chunk * width + start + LANES] = rows.reshape(LANES, 2, LANES)

    def fill(near_list, far_list):
        for out_ref, list_ref in ((to_near_ref, near_list), (to_far_ref, far_list)):
            for entry in range(out_ref.shape[0]):
                out_ref[entry] = table_ref[list_ref[entry]]

    odd = lax.rem(lax.axis_index("dom"), 2)

    @pl.when(odd == 0)
    def _():
        fill(up_ref, down_ref)

    @pl.when(odd == 1)
    def _():
        fill(down_ref, up_ref)


def node_table(snap, send_up, send_down):
    node_count = snap.shape[2]
    halo = send_up.shape[0]
    smem = pl.BlockSpec(memory_space=pltpu.SMEM)
    vmem = pl.BlockSpec(memory_space=pltpu.VMEM)
    chunks = 4 if node_count % (4 * LANES) == 0 else 1
    return pl.pallas_call(
        table_kernel,
        in_specs=[pl.BlockSpec(memory_space=pltpu.HBM), smem, smem],
        out_specs=[vmem] * 3,
        out_shape=[
            jax.ShapeDtypeStruct((node_count, 2, LANES), BF16),
            jax.ShapeDtypeStruct((halo, 2, LANES), BF16),
            jax.ShapeDtypeStruct((halo, 2, LANES), BF16),
        ],
        scratch_shapes=[pltpu.VMEM((chunks, 3, HALF, node_count // chunks), BF16), pltpu.SemaphoreType.DMA((chunks,))],
        compiler_params=pltpu.CompilerParams(vmem_limit_bytes=VMEM_BYTES),
        name="node_table",
    )(*(pltpu.with_memory_space_constraint(operand, pltpu.HBM) for operand in (snap, send_up, send_down)))


def spread_kernel(tile_hbm, out_ref, tile_ref, sem):
    sides = out_ref.shape[0]
    depth = sides * LANES
    groups = LANES // GROUP
    chunks, height, width = tile_ref.shape
    tiles = height // 9
    copies = [
        pltpu.make_async_copy(tile_hbm.at[:, pl.ds(chunk * width, width)], tile_ref.at[chunk], sem.at[chunk])
        for chunk in range(chunks)
    ]
    for copy in copies:
        copy.start()
    row = lax.broadcasted_iota(jnp.int32, (height, depth), 0)
    col = lax.broadcasted_iota(jnp.int32, (height, depth), 1)
    same_tile = row % tiles == col // (2 * GROUP)
    spreads = []
    for half in range(2):
        in_comp = col % 2 if half == 0 else jnp.where(col % 2 == 0, 2, -1)
        for comp in range(3):
            kept = same_tile & (row // tiles == 3 * comp + in_comp) & (in_comp >= 0)
            spreads.append(jnp.where(kept, 1.0, 0.0).astype(BF16))
    node = lax.broadcasted_iota(jnp.int32, (GROUP, depth), 0)
    slot = (lax.broadcasted_iota(jnp.int32, (GROUP, depth), 1) // 2) % GROUP
    own = node == slot
    for chunk in range(chunks):
        copies[chunk].wait()
        for block in range(width // LANES):
            turned = tile_ref[chunk, :, block * LANES : (block + 1) * LANES].T
            first = (chunk * width // LANES + block) * groups
            for pair in range(3):
                both = [jnp.dot(turned, spreads[2 * pair + one], preferred_element_type=F32) for one in range(2)]
                for group in range(groups):
                    kept = [jnp.where(own, part[group * GROUP : (group + 1) * GROUP], 0.0) for part in both]
                    rows = jnp.concatenate(kept, axis=0).astype(BF16)
                    for side in range(sides):
                        out_ref[side, first + group, 16 * pair : 16 * (pair + 1), :] = rows[:, side * LANES : (side + 1) * LANES]


def spread_tiles(mass_tiles):
    tiles, _, _, node_count = mass_tiles.shape
    sides = tiles * GROUP * 2 // LANES
    chunks = 4 if node_count % (4 * LANES) == 0 else 1
    return pl.pallas_call(
        spread_kernel,
        in_specs=[pl.BlockSpec(memory_space=pltpu.HBM)],
        out_specs=pl.BlockSpec(memory_space=pltpu.VMEM),
        out_shape=jax.ShapeDtypeStruct((sides, node_count // GROUP, 48, LANES), BF16),
        scratch_shapes=[pltpu.VMEM((chunks, tiles * 9, node_count // chunks), BF16), pltpu.SemaphoreType.DMA((chunks,))],
        compiler_params=pltpu.CompilerParams(vmem_limit_bytes=VMEM_BYTES),
        cost_estimate=pl.CostEstimate(flops=2 * node_count * tiles * 9 * 6 * sides * LANES, bytes_accessed=node_count * 6 * sides * LANES * 2, transcendentals=0),
        name="spread_tiles",
    )(pltpu.with_memory_space_constraint(jnp.transpose(mass_tiles, (1, 2, 0, 3)).reshape(tiles * 9, node_count), pltpu.HBM))


def mass_kernel(parts, slot_hbm, table_hbm, near_in, far_in, left_ref, own_ref, out_ref, again_ref, *scratch):
    slot_refs = scratch[:parts]
    table_ref, turn_ref, sem, fill_sem = scratch[parts:]
    step, steps = pl.program_id(0), pl.num_programs(0)
    others = slot_hbm.shape[0]
    sides = left_ref.shape[0]
    nodes, halo = table_hbm.shape[0], near_in.shape[0]
    groups = LANES // GROUP
    low_half = lax.broadcasted_iota(jnp.int32, (GROUP, LANES), 1) < HALF

    def fetch(block, part):
        source = slot_hbm.at[:, pl.ds(pl.multiple_of(block * LANES, LANES), LANES)]
        return pltpu.make_async_copy(source, slot_refs[part], sem.at[part])

    @pl.when(step == 0)
    def _():
        odd = lax.rem(lax.axis_index("dom"), 2)
        fills = [
            pltpu.make_async_copy(table_hbm, table_ref.at[pl.ds(0, nodes)], fill_sem.at[0]),
            pltpu.make_async_copy(near_in, table_ref.at[pl.ds(nodes + (1 - odd) * halo, halo)], fill_sem.at[1]),
            pltpu.make_async_copy(far_in, table_ref.at[pl.ds(nodes + odd * halo, halo)], fill_sem.at[2]),
        ]
        for copy in (fetch(0, 0), *fills, *(fetch(part, part) for part in range(1, parts))):
            copy.start()
        for fill in fills:
            fill.wait()

    for part in range(parts):
        block = parts * step + part
        fetch(block, part).wait()
        for group in range(groups):
            rows = [own_ref[pl.ds(pl.multiple_of((block * groups + group) * 2 * GROUP, 2 * GROUP), 2 * GROUP), :]]
            for tile in range(others):
                found = [table_ref[slot_refs[part][tile, group * GROUP + node]] for node in range(GROUP)]
                rows.append(jnp.stack(found).reshape(2 * GROUP, LANES))
            left = jnp.concatenate([left_ref[side, block * groups + group] for side in range(sides)], axis=1)
            sums = jnp.dot(left, jnp.concatenate(rows, axis=0), preferred_element_type=F32)
            for comp in range(3):
                low = sums[comp * GROUP : (comp + 1) * GROUP]
                high = sums[(3 + comp) * GROUP : (4 + comp) * GROUP]
                turn_ref[comp, group * GROUP : (group + 1) * GROUP, :] = jnp.where(low_half, low, high)

        @pl.when(step < steps - 1)
        def _():
            fetch(block + parts, part).start()

        for comp in range(3):
            turned = turn_ref[comp].T
            rounded = (turned[:HALF] + turned[HALF:]).astype(BF16)
            out_ref[comp, :, part * LANES : (part + 1) * LANES] = rounded
            again_ref[comp, :, part * LANES : (part + 1) * LANES] = rounded


def apply_mass(table, from_near, from_far, left, tile_slot):
    nodes, halo = table.shape[0], from_near.shape[0]
    others = tile_slot.shape[0]
    sides = left.shape[0]
    blocks = nodes // LANES
    parts = next(count for count in (4, 2, 1) if blocks % count == 0)
    any_space = pl.BlockSpec(memory_space=pl.ANY)
    return pl.pallas_call(
        functools.partial(mass_kernel, parts),
        grid=(blocks // parts,),
        in_specs=[any_space] * 2 + [pl.BlockSpec(memory_space=pltpu.VMEM)] * 4,
        out_specs=[pl.BlockSpec((3, HALF, parts * LANES), lambda i: (0, 0, i))] * 2,
        out_shape=[jax.ShapeDtypeStruct((3, HALF, nodes), BF16)] * 2,
        scratch_shapes=[pltpu.SMEM((others, LANES), jnp.int32)] * parts
        + [
            pltpu.VMEM((nodes + 2 * halo, 2, LANES), BF16),
            pltpu.VMEM((3, LANES, LANES), F32),
            pltpu.SemaphoreType.DMA((parts,)),
            pltpu.SemaphoreType.DMA((3,)),
        ],
        cost_estimate=pl.CostEstimate(flops=2 * nodes * 6 * sides * LANES * LANES, bytes_accessed=left.size * 2, transcendentals=0),
        compiler_params=pltpu.CompilerParams(vmem_limit_bytes=VMEM_BYTES),
        name="mass_rows",
    )(tile_slot, table, from_near, from_far, left, table.reshape(2 * nodes, LANES))


def summed(value, axis):
    count = lax.axis_size(axis)
    if count & (count - 1):
        return lax.psum(value, axis)
    step = 1
    while step < count:
        value = value + lax.ppermute(value, axis, [(source, source ^ step) for source in range(count)])
        step *= 2
    return value


def in_order(blocks):
    cols, here = len(blocks), lax.axis_index("col")
    if cols == 2:
        first = here == 0
        return jnp.concatenate([jnp.where(first, *blocks), jnp.where(first, *blocks[::-1])], axis=1)
    return jnp.concatenate([lax.dynamic_index_in_dim(jnp.stack(blocks), lax.rem(here - col + cols, cols), 0, False) for col in range(cols)], axis=1)


def body(snapshots, mass_tiles, tile_slot, send_up, send_down):
    snap_count, _, node_count = snapshots.shape
    cols = lax.axis_size("col")
    by_comp = jnp.transpose(snapshots, (1, 0, 2))
    parts = [by_comp]
    for shift in range(1, cols):
        parts.append(lax.ppermute(by_comp, "col", [(source, (source + shift) % cols) for source in range(cols)]))
    left = spread_tiles(mass_tiles)
    pieces = []
    for start in range(0, snap_count, HALF):
        piece = by_comp[:, start : start + HALF]
        size = piece.shape[1]
        if size < HALF:
            piece = jnp.pad(piece, ((0, 0), (0, HALF - size), (0, 0)))
        table, to_near, to_far = node_table(piece, send_up, send_down)
        from_far = swap(to_far, "dom", 1)
        from_near = swap(to_near, "dom", 0)
        both = apply_mass(table, from_near, from_far, left, tile_slot)
        pieces.append([rows[:, :size] for rows in both])
    mass_rows, again = pieces[0] if len(pieces) == 1 else [jnp.concatenate(rows, axis=1) for rows in zip(*pieces)]
    blocks = [lax.dot_general(again, part, (((0, 2), (0, 2)), ((), ())), preferred_element_type=F32) for part in parts]
    total = summed(in_order(blocks), "dom") / (3.0 * node_count * lax.axis_size("dom"))
    return jnp.transpose(mass_rows, (1, 0, 2)), total.T


def solution(mesh):
    placed = (P("col", None, "dom"), P(None, None, None, "dom"), P(None, "dom"), P("dom"), P("dom"))
    return jax.shard_map(
        body,
        mesh=mesh,
        in_specs=placed,
        out_specs=(P("col", None, "dom"), P(None, "col")),
        check_vma=False,
    )
```

```python
import functools

import jax
import jax.numpy as jnp
from jax import lax
from jax.experimental import pallas as pl
from jax.experimental.pallas import tpu as pltpu
from jax.sharding import PartitionSpec as P

LANES = 128
HALF = LANES // 2
GROUP = 8
VMEM_BYTES = 20 * 2**20
BF16 = jnp.bfloat16
F32 = jnp.float32


def swap(value, axis, first):
    count = lax.axis_size(axis)
    pairs = [(low, low + 1) for low in range(first, count - 1, 2)]
    return lax.ppermute(value, axis, pairs + [(high, low) for low, high in pairs])


def nt_dot(left, right):
    return lax.dot_general(left, right, (((1,), (1,)), ((), ())), preferred_element_type=F32)


def table_kernel(snap_hbm, up_ref, down_ref, table_ref, to_near_ref, to_far_ref, snap_ref, sem):
    chunks = snap_ref.shape[0]
    width = snap_ref.shape[3]
    copies = [
        pltpu.make_async_copy(snap_hbm.at[:, :, pl.ds(chunk * width, width)], snap_ref.at[chunk], sem.at[chunk])
        for chunk in range(chunks)
    ]
    for copy in copies:
        copy.start()
    row = lax.broadcasted_iota(jnp.int32, (2 * LANES, 2 * LANES), 0)
    col = lax.broadcasted_iota(jnp.int32, (2 * LANES, 2 * LANES), 1)
    pick = jnp.where(col == (row // 2) + LANES * (row % 2), 1.0, 0.0).astype(BF16)
    empty = jnp.zeros((HALF, LANES), BF16)
    for chunk in range(chunks):
        copies[chunk].wait()
        for start in range(0, width, LANES):
            comps = [snap_ref[chunk, comp, :, start : start + LANES] for comp in range(3)]
            first = jnp.concatenate([comps[0], comps[2]], axis=0)
            second = jnp.concatenate([comps[1], empty], axis=0)
            rows = nt_dot(pick, jnp.concatenate([first, second], axis=1)).astype(BF16)
            table_ref[chunk * width + start : chunk * width + start + LANES] = rows.reshape(LANES, 2, LANES)

    def fill(near_list, far_list):
        for out_ref, list_ref in ((to_near_ref, near_list), (to_far_ref, far_list)):
            for entry in range(out_ref.shape[0]):
                out_ref[entry] = table_ref[list_ref[entry]]

    odd = lax.rem(lax.axis_index("dom"), 2)

    @pl.when(odd == 0)
    def _():
        fill(up_ref, down_ref)

    @pl.when(odd == 1)
    def _():
        fill(down_ref, up_ref)


def node_table(snap, send_up, send_down):
    node_count = snap.shape[2]
    halo = send_up.shape[0]
    smem = pl.BlockSpec(memory_space=pltpu.SMEM)
    vmem = pl.BlockSpec(memory_space=pltpu.VMEM)
    chunks = 4 if node_count % (4 * LANES) == 0 else 1
    return pl.pallas_call(
        table_kernel,
        in_specs=[pl.BlockSpec(memory_space=pltpu.HBM), smem, smem],
        out_specs=[vmem] * 3,
        out_shape=[
            jax.ShapeDtypeStruct((node_count, 2, LANES), BF16),
            jax.ShapeDtypeStruct((halo, 2, LANES), BF16),
            jax.ShapeDtypeStruct((halo, 2, LANES), BF16),
        ],
        scratch_shapes=[pltpu.VMEM((chunks, 3, HALF, node_count // chunks), BF16), pltpu.SemaphoreType.DMA((chunks,))],
        compiler_params=pltpu.CompilerParams(vmem_limit_bytes=VMEM_BYTES),
        name="node_table",
    )(*(pltpu.with_memory_space_constraint(operand, pltpu.HBM) for operand in (snap, send_up, send_down)))


def spread_kernel(tile_hbm, out_ref, tile_ref, sem):
    sides = out_ref.shape[0]
    depth = sides * LANES
    groups = LANES // GROUP
    chunks, height, width = tile_ref.shape
    tiles = height // 9
    copies = [
        pltpu.make_async_copy(tile_hbm.at[:, pl.ds(chunk * width, width)], tile_ref.at[chunk], sem.at[chunk])
        for chunk in range(chunks)
    ]
    for copy in copies:
        copy.start()
    row = lax.broadcasted_iota(jnp.int32, (height, depth), 0)
    col = lax.broadcasted_iota(jnp.int32, (height, depth), 1)
    same_tile = row % tiles == col // (2 * GROUP)
    spreads = []
    for half in range(2):
        in_comp = col % 2 if half == 0 else jnp.where(col % 2 == 0, 2, -1)
        for comp in range(3):
            kept = same_tile & (row // tiles == 3 * comp + in_comp) & (in_comp >= 0)
            spreads.append(jnp.where(kept, 1.0, 0.0).astype(BF16))
    node = lax.broadcasted_iota(jnp.int32, (GROUP, depth), 0)
    slot = (lax.broadcasted_iota(jnp.int32, (GROUP, depth), 1) // 2) % GROUP
    own = node == slot
    for chunk in range(chunks):
        copies[chunk].wait()
        for block in range(width // LANES):
            turned = tile_ref[chunk, :, block * LANES : (block + 1) * LANES].T
            first = (chunk * width // LANES + block) * groups
            for pair in range(3):
                both = [jnp.dot(turned, spreads[2 * pair + one], preferred_element_type=F32) for one in range(2)]
                for group in range(groups):
                    kept = [jnp.where(own, part[group * GROUP : (group + 1) * GROUP], 0.0) for part in both]
                    rows = jnp.concatenate(kept, axis=0).astype(BF16)
                    for side in range(sides):
                        out_ref[side, first + group, 16 * pair : 16 * (pair + 1), :] = rows[:, side * LANES : (side + 1) * LANES]


def spread_tiles(mass_tiles):
    tiles, _, _, node_count = mass_tiles.shape
    sides = tiles * GROUP * 2 // LANES
    chunks = 4 if node_count % (4 * LANES) == 0 else 1
    return pl.pallas_call(
        spread_kernel,
        in_specs=[pl.BlockSpec(memory_space=pltpu.HBM)],
        out_specs=pl.BlockSpec(memory_space=pltpu.VMEM),
        out_shape=jax.ShapeDtypeStruct((sides, node_count // GROUP, 48, LANES), BF16),
        scratch_shapes=[pltpu.VMEM((chunks, tiles * 9, node_count // chunks), BF16), pltpu.SemaphoreType.DMA((chunks,))],
        compiler_params=pltpu.CompilerParams(vmem_limit_bytes=VMEM_BYTES),
        cost_estimate=pl.CostEstimate(flops=2 * node_count * tiles * 9 * 6 * sides * LANES, bytes_accessed=node_count * 6 * sides * LANES * 2, transcendentals=0),
        name="spread_tiles",
    )(pltpu.with_memory_space_constraint(jnp.transpose(mass_tiles, (1, 2, 0, 3)).reshape(tiles * 9, node_count), pltpu.HBM))


def mass_kernel(parts, slot_hbm, table_hbm, near_in, far_in, left_ref, own_ref, out_ref, again_ref, *scratch):
    slot_refs = scratch[:parts]
    table_ref, turn_ref, sem, fill_sem = scratch[parts:]
    step, steps = pl.program_id(0), pl.num_programs(0)
    others = slot_hbm.shape[0]
    sides = left_ref.shape[0]
    nodes, halo = table_hbm.shape[0], near_in.shape[0]
    groups = LANES // GROUP
    low_half = lax.broadcasted_iota(jnp.int32, (GROUP, LANES), 1) < HALF

    def fetch(block, part):
        source = slot_hbm.at[:, pl.ds(pl.multiple_of(block * LANES, LANES), LANES)]
        return pltpu.make_async_copy(source, slot_refs[part], sem.at[part])

    @pl.when(step == 0)
    def _():
        odd = lax.rem(lax.axis_index("dom"), 2)
        fills = [
            pltpu.make_async_copy(table_hbm, table_ref.at[pl.ds(0, nodes)], fill_sem.at[0]),
            pltpu.make_async_copy(near_in, table_ref.at[pl.ds(nodes + (1 - odd) * halo, halo)], fill_sem.at[1]),
            pltpu.make_async_copy(far_in, table_ref.at[pl.ds(nodes + odd * halo, halo)], fill_sem.at[2]),
        ]
        for copy in (fetch(0, 0), *fills, *(fetch(part, part) for part in range(1, parts))):
            copy.start()
        for fill in fills:
            fill.wait()

    def flush(part):
        for comp in range(3):
            turned = turn_ref[part % 2, comp].T
            rounded = (turned[:HALF] + turned[HALF:]).astype(BF16)
            out_ref[comp, :, part * LANES : (part + 1) * LANES] = rounded
            again_ref[comp, :, part * LANES : (part + 1) * LANES] = rounded

    for part in range(parts):
        block = parts * step + part
        fetch(block, part).wait()
        if part:
            flush(part - 1)
        for group in range(groups):
            rows = [own_ref[pl.ds(pl.multiple_of((block * groups + group) * 2 * GROUP, 2 * GROUP), 2 * GROUP), :]]
            for tile in range(others):
                found = [table_ref[slot_refs[part][tile, group * GROUP + node]] for node in range(GROUP)]
                rows.append(jnp.stack(found).reshape(2 * GROUP, LANES))
            left = jnp.concatenate([left_ref[side, block * groups + group] for side in range(sides)], axis=1)
            sums = jnp.dot(left, jnp.concatenate(rows, axis=0), preferred_element_type=F32)
            for comp in range(3):
                low = sums[comp * GROUP : (comp + 1) * GROUP]
                high = sums[(3 + comp) * GROUP : (4 + comp) * GROUP]
                turn_ref[part % 2, comp, group * GROUP : (group + 1) * GROUP, :] = jnp.where(low_half, low, high)

        @pl.when(step < steps - 1)
        def _():
            fetch(block + parts, part).start()

    flush(parts - 1)


def apply_mass(table, from_near, from_far, left, tile_slot):
    nodes, halo = table.shape[0], from_near.shape[0]
    others = tile_slot.shape[0]
    sides = left.shape[0]
    blocks = nodes // LANES
    parts = next(count for count in (8, 4, 2, 1) if blocks % count == 0)
    any_space = pl.BlockSpec(memory_space=pl.ANY)
    return pl.pallas_call(
        functools.partial(mass_kernel, parts),
        grid=(blocks // parts,),
        in_specs=[any_space] * 2 + [pl.BlockSpec(memory_space=pltpu.VMEM)] * 4,
        out_specs=[pl.BlockSpec((3, HALF, parts * LANES), lambda i: (0, 0, i))] * 2,
        out_shape=[jax.ShapeDtypeStruct((3, HALF, nodes), BF16)] * 2,
        scratch_shapes=[pltpu.SMEM((others, LANES), jnp.int32)] * parts
        + [
            pltpu.VMEM((nodes + 2 * halo, 2, LANES), BF16),
            pltpu.VMEM((2, 3, LANES, LANES), F32),
            pltpu.SemaphoreType.DMA((parts,)),
            pltpu.SemaphoreType.DMA((3,)),
        ],
        cost_estimate=pl.CostEstimate(flops=2 * nodes * 6 * sides * LANES * LANES, bytes_accessed=left.size * 2, transcendentals=0),
        compiler_params=pltpu.CompilerParams(vmem_limit_bytes=VMEM_BYTES),
        name="mass_rows",
    )(tile_slot, table, from_near, from_far, left, table.reshape(2 * nodes, LANES))


def summed(value, axis):
    count = lax.axis_size(axis)
    if count & (count - 1):
        return lax.psum(value, axis)
    step = 1
    while step < count:
        value = value + lax.ppermute(value, axis, [(source, source ^ step) for source in range(count)])
        step *= 2
    return value


def in_order(blocks):
    cols, here = len(blocks), lax.axis_index("col")
    if cols == 2:
        first = here == 0
        return jnp.concatenate([jnp.where(first, *blocks), jnp.where(first, *blocks[::-1])], axis=1)
    return jnp.concatenate([lax.dynamic_index_in_dim(jnp.stack(blocks), lax.rem(here - col + cols, cols), 0, False) for col in range(cols)], axis=1)


def body(snapshots, mass_tiles, tile_slot, send_up, send_down):
    snap_count, _, node_count = snapshots.shape
    cols = lax.axis_size("col")
    by_comp = jnp.transpose(snapshots, (1, 0, 2))
    parts = [by_comp]
    for shift in range(1, cols):
        parts.append(lax.ppermute(by_comp, "col", [(source, (source + shift) % cols) for source in range(cols)]))
    left = spread_tiles(mass_tiles)
    pieces = []
    for start in range(0, snap_count, HALF):
        piece = by_comp[:, start : start + HALF]
        size = piece.shape[1]
        if size < HALF:
            piece = jnp.pad(piece, ((0, 0), (0, HALF - size), (0, 0)))
        table, to_near, to_far = node_table(piece, send_up, send_down)
        from_far = swap(to_far, "dom", 1)
        from_near = swap(to_near, "dom", 0)
        both = apply_mass(table, from_near, from_far, left, tile_slot)
        pieces.append([rows[:, :size] for rows in both])
    mass_rows, again = pieces[0] if len(pieces) == 1 else [jnp.concatenate(rows, axis=1) for rows in zip(*pieces)]
    blocks = [lax.dot_general(again, part, (((0, 2), (0, 2)), ((), ())), preferred_element_type=F32) for part in parts]
    total = summed(in_order(blocks), "dom") / (3.0 * node_count * lax.axis_size("dom"))
    return jnp.transpose(mass_rows, (1, 0, 2)), total.T


def solution(mesh):
    placed = (P("col", None, "dom"), P(None, None, None, "dom"), P(None, "dom"), P("dom"), P("dom"))
    return jax.shard_map(
        body,
        mesh=mesh,
        in_specs=placed,
        out_specs=(P("col", None, "dom"), P(None, "col")),
        check_vma=False,
    )
```

```python
import functools

import jax
import jax.numpy as jnp
from jax import lax
from jax.experimental import pallas as pl
from jax.experimental.pallas import tpu as pltpu
from jax.sharding import PartitionSpec as P

LANES = 128
HALF = LANES // 2
GROUP = 8
VMEM_BYTES = 20 * 2**20
BF16 = jnp.bfloat16
F32 = jnp.float32


def swap(value, axis, first):
    count = lax.axis_size(axis)
    pairs = [(low, low + 1) for low in range(first, count - 1, 2)]
    return lax.ppermute(value, axis, pairs + [(high, low) for low, high in pairs])


def nt_dot(left, right):
    return lax.dot_general(left, right, (((1,), (1,)), ((), ())), preferred_element_type=F32)


def table_kernel(snap_hbm, up_hbm, down_hbm, table_ref, to_near_ref, to_far_ref, snap_ref, up_ref, down_ref, sem, list_sem):
    chunks = snap_ref.shape[0]
    width = snap_ref.shape[3]
    copies = [
        pltpu.make_async_copy(snap_hbm.at[:, :, pl.ds(chunk * width, width)], snap_ref.at[chunk], sem.at[chunk])
        for chunk in range(chunks)
    ]
    lists = [pltpu.make_async_copy(up_hbm, up_ref, list_sem.at[0]), pltpu.make_async_copy(down_hbm, down_ref, list_sem.at[1])]
    for copy in copies + lists:
        copy.start()
    row = lax.broadcasted_iota(jnp.int32, (2 * LANES, 2 * LANES), 0)
    col = lax.broadcasted_iota(jnp.int32, (2 * LANES, 2 * LANES), 1)
    pick = jnp.where(col == (row // 2) + LANES * (row % 2), 1.0, 0.0).astype(BF16)
    empty = jnp.zeros((HALF, LANES), BF16)
    for chunk in range(chunks):
        copies[chunk].wait()
        for start in range(0, width, LANES):
            comps = [snap_ref[chunk, comp, :, start : start + LANES] for comp in range(3)]
            first = jnp.concatenate([comps[0], comps[2]], axis=0)
            second = jnp.concatenate([comps[1], empty], axis=0)
            rows = nt_dot(pick, jnp.concatenate([first, second], axis=1)).astype(BF16)
            table_ref[chunk * width + start : chunk * width + start + LANES] = rows.reshape(LANES, 2, LANES)

    for copy in lists:
        copy.wait()

    def fill(near_list, far_list):
        for out_ref, list_ref in ((to_near_ref, near_list), (to_far_ref, far_list)):
            for entry in range(out_ref.shape[0]):
                out_ref[entry] = table_ref[list_ref[entry]]

    odd = lax.rem(lax.axis_index("dom"), 2)

    @pl.when(odd == 0)
    def _():
        fill(up_ref, down_ref)

    @pl.when(odd == 1)
    def _():
        fill(down_ref, up_ref)


def node_table(snap, send_up, send_down):
    node_count = snap.shape[2]
    halo = send_up.shape[0]
    hbm = pl.BlockSpec(memory_space=pltpu.HBM)
    vmem = pl.BlockSpec(memory_space=pltpu.VMEM)
    chunks = 4 if node_count % (4 * LANES) == 0 else 1
    return pl.pallas_call(
        table_kernel,
        in_specs=[hbm] * 3,
        out_specs=[vmem] * 3,
        out_shape=[
            jax.ShapeDtypeStruct((node_count, 2, LANES), BF16),
            jax.ShapeDtypeStruct((halo, 2, LANES), BF16),
            jax.ShapeDtypeStruct((halo, 2, LANES), BF16),
        ],
        scratch_shapes=[
            pltpu.VMEM((chunks, 3, HALF, node_count // chunks), BF16),
            pltpu.SMEM((halo,), jnp.int32),
            pltpu.SMEM((halo,), jnp.int32),
            pltpu.SemaphoreType.DMA((chunks,)),
            pltpu.SemaphoreType.DMA((2,)),
        ],
        compiler_params=pltpu.CompilerParams(vmem_limit_bytes=VMEM_BYTES),
        name="node_table",
    )(*(pltpu.with_memory_space_constraint(operand, pltpu.HBM) for operand in (snap, send_up, send_down)))


def spread_kernel(tile_hbm, out_ref, tile_ref, sem):
    sides = out_ref.shape[0]
    depth = sides * LANES
    groups = LANES // GROUP
    chunks, height, width = tile_ref.shape
    tiles = height // 9
    copies = [
        pltpu.make_async_copy(tile_hbm.at[:, pl.ds(chunk * width, width)], tile_ref.at[chunk], sem.at[chunk])
        for chunk in range(chunks)
    ]
    for copy in copies:
        copy.start()
    row = lax.broadcasted_iota(jnp.int32, (height, depth), 0)
    col = lax.broadcasted_iota(jnp.int32, (height, depth), 1)
    same_tile = row % tiles == col // (2 * GROUP)
    spreads = []
    for half in range(2):
        in_comp = col % 2 if half == 0 else jnp.where(col % 2 == 0, 2, -1)
        for comp in range(3):
            kept = same_tile & (row // tiles == 3 * comp + in_comp) & (in_comp >= 0)
            spreads.append(jnp.where(kept, 1.0, 0.0).astype(BF16))
    node = lax.broadcasted_iota(jnp.int32, (GROUP, depth), 0)
    slot = (lax.broadcasted_iota(jnp.int32, (GROUP, depth), 1) // 2) % GROUP
    own = node == slot
    for chunk in range(chunks):
        copies[chunk].wait()
        for block in range(width // LANES):
            turned = tile_ref[chunk, :, block * LANES : (block + 1) * LANES].T
            first = (chunk * width // LANES + block) * groups
            for pair in range(3):
                both = [jnp.dot(turned, spreads[2 * pair + one], preferred_element_type=F32) for one in range(2)]
                for group in range(groups):
                    kept = [jnp.where(own, part[group * GROUP : (group + 1) * GROUP], 0.0) for part in both]
                    rows = jnp.concatenate(kept, axis=0).astype(BF16)
                    for side in range(sides):
                        out_ref[side, first + group, 16 * pair : 16 * (pair + 1), :] = rows[:, side * LANES : (side + 1) * LANES]


def spread_tiles(mass_tiles):
    tiles, _, _, node_count = mass_tiles.shape
    sides = tiles * GROUP * 2 // LANES
    chunks = 4 if node_count % (4 * LANES) == 0 else 1
    return pl.pallas_call(
        spread_kernel,
        in_specs=[pl.BlockSpec(memory_space=pltpu.HBM)],
        out_specs=pl.BlockSpec(memory_space=pltpu.VMEM),
        out_shape=jax.ShapeDtypeStruct((sides, node_count // GROUP, 48, LANES), BF16),
        scratch_shapes=[pltpu.VMEM((chunks, tiles * 9, node_count // chunks), BF16), pltpu.SemaphoreType.DMA((chunks,))],
        compiler_params=pltpu.CompilerParams(vmem_limit_bytes=VMEM_BYTES),
        cost_estimate=pl.CostEstimate(flops=2 * node_count * tiles * 9 * 6 * sides * LANES, bytes_accessed=node_count * 6 * sides * LANES * 2, transcendentals=0),
        name="spread_tiles",
    )(pltpu.with_memory_space_constraint(jnp.transpose(mass_tiles, (1, 2, 0, 3)).reshape(tiles * 9, node_count), pltpu.HBM))


def mass_kernel(parts, slot_hbm, table_hbm, near_in, far_in, left_ref, own_ref, out_ref, again_ref, *scratch):
    slot_refs = scratch[:parts]
    table_ref, turn_ref, sem, fill_sem = scratch[parts:]
    step, steps = pl.program_id(0), pl.num_programs(0)
    others = slot_hbm.shape[0]
    sides = left_ref.shape[0]
    nodes, halo = table_hbm.shape[0], near_in.shape[0]
    groups = LANES // GROUP
    low_half = lax.broadcasted_iota(jnp.int32, (GROUP, LANES), 1) < HALF

    def fetch(block, part):
        source = slot_hbm.at[:, pl.ds(pl.multiple_of(block * LANES, LANES), LANES)]
        return pltpu.make_async_copy(source, slot_refs[part], sem.at[part])

    @pl.when(step == 0)
    def _():
        odd = lax.rem(lax.axis_index("dom"), 2)
        fills = [
            pltpu.make_async_copy(table_hbm, table_ref.at[pl.ds(0, nodes)], fill_sem.at[0]),
            pltpu.make_async_copy(near_in, table_ref.at[pl.ds(nodes + (1 - odd) * halo, halo)], fill_sem.at[1]),
            pltpu.make_async_copy(far_in, table_ref.at[pl.ds(nodes + odd * halo, halo)], fill_sem.at[2]),
        ]
        for copy in (fetch(0, 0), *fills, *(fetch(part, part) for part in range(1, parts))):
            copy.start()
        for fill in fills:
            fill.wait()

    def flush(part):
        for comp in range(3):
            turned = turn_ref[part % 2, comp].T
            rounded = (turned[:HALF] + turned[HALF:]).astype(BF16)
            out_ref[comp, :, part * LANES : (part + 1) * LANES] = rounded
            again_ref[comp, :, part * LANES : (part + 1) * LANES] = rounded

    for part in range(parts):
        block = parts * step + part
        fetch(block, part).wait()
        if part:
            flush(part - 1)
        for group in range(groups):
            rows = [own_ref[pl.ds(pl.multiple_of((block * groups + group) * 2 * GROUP, 2 * GROUP), 2 * GROUP), :]]
            for tile in range(others):
                found = [table_ref[slot_refs[part][tile, group * GROUP + node]] for node in range(GROUP)]
                rows.append(jnp.stack(found).reshape(2 * GROUP, LANES))
            left = jnp.concatenate([left_ref[side, block * groups + group] for side in range(sides)], axis=1)
            sums = jnp.dot(left, jnp.concatenate(rows, axis=0), preferred_element_type=F32)
            for comp in range(3):
                low = sums[comp * GROUP : (comp + 1) * GROUP]
                high = sums[(3 + comp) * GROUP : (4 + comp) * GROUP]
                turn_ref[part % 2, comp, group * GROUP : (group + 1) * GROUP, :] = jnp.where(low_half, low, high)

        @pl.when(step < steps - 1)
        def _():
            fetch(block + parts, part).start()

    flush(parts - 1)


def apply_mass(table, from_near, from_far, left, tile_slot):
    nodes, halo = table.shape[0], from_near.shape[0]
    others = tile_slot.shape[0]
    sides = left.shape[0]
    blocks = nodes // LANES
    parts = next(count for count in (8, 4, 2, 1) if blocks % count == 0)
    any_space = pl.BlockSpec(memory_space=pl.ANY)
    return pl.pallas_call(
        functools.partial(mass_kernel, parts),
        grid=(blocks // parts,),
        in_specs=[any_space] * 2 + [pl.BlockSpec(memory_space=pltpu.VMEM)] * 4,
        out_specs=[pl.BlockSpec((3, HALF, parts * LANES), lambda i: (0, 0, i))] * 2,
        out_shape=[jax.ShapeDtypeStruct((3, HALF, nodes), BF16)] * 2,
        scratch_shapes=[pltpu.SMEM((others, LANES), jnp.int32)] * parts
        + [
            pltpu.VMEM((nodes + 2 * halo, 2, LANES), BF16),
            pltpu.VMEM((2, 3, LANES, LANES), F32),
            pltpu.SemaphoreType.DMA((parts,)),
            pltpu.SemaphoreType.DMA((3,)),
        ],
        cost_estimate=pl.CostEstimate(flops=2 * nodes * 6 * sides * LANES * LANES, bytes_accessed=left.size * 2, transcendentals=0),
        compiler_params=pltpu.CompilerParams(vmem_limit_bytes=VMEM_BYTES),
        name="mass_rows",
    )(tile_slot, table, from_near, from_far, left, table.reshape(2 * nodes, LANES))


def summed(value, axis):
    count = lax.axis_size(axis)
    if count & (count - 1):
        return lax.psum(value, axis)
    step = 1
    while step < count:
        value = value + lax.ppermute(value, axis, [(source, source ^ step) for source in range(count)])
        step *= 2
    return value


def in_order(blocks):
    cols, here = len(blocks), lax.axis_index("col")
    if cols == 2:
        first = here == 0
        return jnp.concatenate([jnp.where(first, *blocks), jnp.where(first, *blocks[::-1])], axis=1)
    return jnp.concatenate([lax.dynamic_index_in_dim(jnp.stack(blocks), lax.rem(here - col + cols, cols), 0, False) for col in range(cols)], axis=1)


def body(snapshots, mass_tiles, tile_slot, send_up, send_down):
    snap_count, _, node_count = snapshots.shape
    cols = lax.axis_size("col")
    by_comp = jnp.transpose(snapshots, (1, 0, 2))
    parts = [by_comp]
    for shift in range(1, cols):
        parts.append(lax.ppermute(by_comp, "col", [(source, (source + shift) % cols) for source in range(cols)]))
    left = spread_tiles(mass_tiles)
    pieces = []
    for start in range(0, snap_count, HALF):
        piece = by_comp[:, start : start + HALF]
        size = piece.shape[1]
        if size < HALF:
            piece = jnp.pad(piece, ((0, 0), (0, HALF - size), (0, 0)))
        table, to_near, to_far = node_table(piece, send_up, send_down)
        from_far = swap(to_far, "dom", 1)
        from_near = swap(to_near, "dom", 0)
        both = apply_mass(table, from_near, from_far, left, tile_slot)
        pieces.append([rows[:, :size] for rows in both])
    mass_rows, again = pieces[0] if len(pieces) == 1 else [jnp.concatenate(rows, axis=1) for rows in zip(*pieces)]
    blocks = [lax.dot_general(again, part, (((0, 2), (0, 2)), ((), ())), preferred_element_type=F32) for part in parts]
    total = summed(in_order(blocks), "dom") / (3.0 * node_count * lax.axis_size("dom"))
    return jnp.transpose(mass_rows, (1, 0, 2)), total.T


def solution(mesh):
    placed = (P("col", None, "dom"), P(None, None, None, "dom"), P(None, "dom"), P("dom"), P("dom"))
    return jax.shard_map(
        body,
        mesh=mesh,
        in_specs=placed,
        out_specs=(P("col", None, "dom"), P(None, "col")),
        check_vma=False,
    )
```
